32 devices in a mesh: dp: 8 (over z, x), tile: 4 (over y, core).
Axes of the slice: x: 2, y: 2, z: 4, core: 2. Of those that a mesh axis runs over, the one named last changes fastest.
Arguments:
- frames: bfloat16 [32, 4, 64, 256], P('dp', 'tile'), may hold values from -6 to 6
- kernels: bfloat16 [32, 9, 256, 256], P('dp'), may hold values from -0.125 to 0.125
- experts: int32 [32, 4, 4], P('dp', 'tile'), may hold values from 0 to 31, as said below
- counts: int32 [32, 4], P('dp', 'tile'), may hold values from 2 to 4
- gate_weights: float32 [32, 4, 4], P('dp', 'tile'), may hold values from 0.25 to 1
- cotangent: bfloat16 [32, 4, 64, 256], P('dp', 'tile'), may hold values from -6 to 6
Outputs:
- frames_out: bfloat16 [32, 4, 64, 256], P('dp', 'tile')
- input_grad: bfloat16 [32, 4, 64, 256], P('dp', 'tile')
- gate_grad: float32 [32, 4, 4], P('dp', 'tile')
- kernel_grad: float32 [32, 9, 256, 256], P('dp', None, None, 'tile')
The draws below stay inside these ranges and needn't reach their ends.
Inputs may be any that keep to these rules, and one draw needn't show every extreme that they name: A tile's 4 experts have distinct values of id // 4. Among the 4 tiles of one device (frames d * 4 to (d + 1) * 4 - 1 at one tile index), each value of id // 4 is named by at most 2 tiles, by exactly 2 for some, and all its slots there name the same id. A tile uses its first counts slots; later slots are ignored.
All inputs are finite; a program needn't handle non-finite values.
Results may differ from the reference program's by a relative error of at most 0.005.
Values may be sent and summed in bfloat16 or wider, within the bound.
A program may use at most 256 MiB of HBM per device.

```python
import jax
import jax.numpy as jnp
from jax import lax

CHANNELS = 256
EXP_DEV = 4
SLOTS = 4
FR_DEV = 4
CAP = 2
TILE_ROWS = 1
TILE_COLS = 64
EXPERTS = 32
BATCH = 32
HEIGHT = 4
N_DP = 8
N_TILE = 4


def draw_experts(key, part):
    groups = N_DP * N_TILE
    listed = FR_DEV * SLOTS // CAP
    stride = SLOTS // CAP
    first, second, third, fourth = jax.random.split(key, 4)
    specialist_order = jax.random.permutation(first, N_DP)
    affinity_increment = jnp.maximum(0, 3 - specialist_order)
    stochastic_perturbation = jax.random.randint(second, (groups, N_DP), 0, 4)
    order_keys = jax.random.split(third, groups)
    equality_resolver = jax.vmap(lambda single: jax.random.permutation(single, N_DP))(order_keys)
    specialist_affinity = (stochastic_perturbation + affinity_increment[None, :]) * N_DP + equality_resolver
    listing = lax.top_k(specialist_affinity, listed)[1]
    spots = (jnp.arange(FR_DEV)[:, None] * stride + jnp.arange(SLOTS)[None, :]) % listed
    owners = listing[:, spots]
    local_ids = jax.random.randint(fourth, (groups, N_DP), 0, EXP_DEV)
    taken = jnp.take_along_axis(local_ids, owners.reshape(groups, FR_DEV * SLOTS), axis=1).reshape(owners.shape)
    ids = (owners * EXP_DEV + taken).astype(jnp.int32)
    ids = ids.reshape(N_DP, N_TILE, FR_DEV, SLOTS).transpose(0, 2, 1, 3)
    return ids.reshape(N_DP * FR_DEV, N_TILE, SLOTS)


def set_ends(values, own_key, smallest, high):
    place = [jax.random.randint(jax.random.fold_in(own_key, axis), (), 0, length) for axis, length in enumerate(values.shape)]
    main_axis = values.shape.index(max(values.shape))
    next_to = place[:main_axis] + [(place[main_axis] + 1) % values.shape[main_axis]] + place[main_axis + 1:]
    return values.at[tuple(place)].set(smallest).at[tuple(next_to)].set(high)


def levels(own_key, shape, cuts, smallest, top_value):
    factor_of = 1.0
    for dim, shards_of in cuts:
        draws = jax.random.uniform(jax.random.fold_in(jax.random.fold_in(own_key, 6), dim), (shards_of,), jnp.float32, smallest / len(cuts), top_value / len(cuts))
        factor_of = factor_of * jnp.repeat(jnp.exp(draws), shape[dim] // shards_of).reshape((-1,) + (1,) * (len(shape) - 1 - dim))
    return factor_of


def bell_draw(key, shape, spread, most, cuts=(), held_as=jnp.bfloat16):
    drawn = jax.random.normal(key, shape, jnp.float32) * spread
    if len(cuts) > 0:
        drawn = levels(key, shape, cuts, -0.22, 0.18) * drawn
    return jnp.clip(drawn, min=-most, max=most).astype(held_as)


def setup_inputs(seed: int = 0) -> dict:
    seeds = jax.random.split(jax.random.key(seed), 7)
    return {
        "frames": bell_draw(seeds[0], (BATCH, HEIGHT, TILE_COLS, CHANNELS), 1.0, 6.0, ((0, 8), (1, 4))),
        "kernels": bell_draw(seeds[1], (EXPERTS, 9, CHANNELS, CHANNELS), (9 * CHANNELS) ** -0.5, 0.125, ((0, 8),)),
        "experts": draw_experts(jax.random.fold_in(seeds[6], 71), 0),
        "counts": set_ends(jax.random.randint(seeds[3], (BATCH, N_TILE), 2, SLOTS + 1), jax.random.fold_in(seeds[3], 1), 2, SLOTS).astype(jnp.int32),
        "gate_weights": jnp.clip(0.25 + 0.75 * jax.random.uniform(seeds[4], (BATCH, N_TILE, SLOTS), jnp.float32) ** levels(seeds[4], (BATCH, N_TILE, SLOTS), ((0, 8), (1, 4)), -0.2, 0.2), 0.25, 1.0),
        "cotangent": bell_draw(seeds[5], (BATCH, HEIGHT, TILE_COLS, CHANNELS), 1.0, 6.0, ((0, 8), (1, 4))),
    }


def convolve(window, kernel_weight):
    number_of_rows = window.shape[0] - 2
    columns = window.shape[1]
    widened = jnp.pad(window, ((0, 0), (1, 1), (0, 0)))
    total = jnp.zeros((number_of_rows * columns, kernel_weight.shape[2]), jnp.float32)
    for row_off in range(3):
        for col_off in range(3):
            patch = widened[row_off:row_off + number_of_rows, col_off:col_off + columns].reshape(number_of_rows * columns, -1)
            total = total + jnp.dot(patch, kernel_weight[3 * row_off + col_off], preferred_element_type=jnp.float32)
    return total.reshape(number_of_rows, columns, -1)


def transpose_conv(grad_out, kernel_weight):
    number_of_rows = grad_out.shape[0]
    columns = grad_out.shape[1]
    widened = jnp.pad(grad_out, ((2, 2), (1, 1), (0, 0)))
    total = jnp.zeros(((number_of_rows + 2) * columns, kernel_weight.shape[1]), jnp.float32)
    for row_off in range(3):
        for col_off in range(3):
            patch = widened[2 - row_off:4 - row_off + number_of_rows, 2 - col_off:2 - col_off + columns].reshape((number_of_rows + 2) * columns, -1)
            total = total + lax.dot_general(patch, kernel_weight[3 * row_off + col_off], (((1,), (1,)), ((), ())), preferred_element_type=jnp.float32)
    return total.reshape(number_of_rows + 2, columns, -1)


def kernel_terms(window, grad_out):
    number_of_rows = grad_out.shape[0]
    columns = grad_out.shape[1]
    widened = jnp.pad(window, ((0, 0), (1, 1), (0, 0)))
    flat_grad = grad_out.reshape(number_of_rows * columns, -1)
    pieces = []
    for row_off in range(3):
        for col_off in range(3):
            patch = widened[row_off:row_off + number_of_rows, col_off:col_off + columns].reshape(number_of_rows * columns, -1)
            pieces.append(lax.dot_general(patch, flat_grad, (((0,), (0,)), ((), ())), preferred_element_type=jnp.float32))
    return jnp.stack(pieces)


def activation(pre):
    squash = jax.nn.sigmoid(pre)
    return pre * squash, squash * (1.0 + pre * (1.0 - squash))


def reference(frames, kernels, experts, counts, gate_weights, cotangent):
    padded_frames = jnp.pad(frames, ((0, 0), (1, 1), (0, 0), (0, 0)))
    width = frames.shape[2]
    channels = frames.shape[3]

    def advance(carry, index):
        kernel_grad, grad_frame = carry
        frame_index = index // N_TILE
        place_index = index % N_TILE
        first_row = (place_index * TILE_ROWS).astype(jnp.int32)
        anchor = jnp.zeros((), jnp.int32)
        window = lax.dynamic_slice(padded_frames, (frame_index, first_row, anchor, anchor), (1, TILE_ROWS + 2, width, channels))[0]
        upstream = lax.dynamic_slice(cotangent, (frame_index, first_row, anchor, anchor), (1, TILE_ROWS, width, channels))[0].astype(jnp.float32)
        chosen = experts[frame_index, place_index]
        active_count = counts[frame_index, place_index]
        gate_row = gate_weights[frame_index, place_index]
        result = window[1:-1].astype(jnp.float32)
        rim_sum = jnp.zeros((TILE_ROWS + 2, width, channels), jnp.float32)
        gate_terms = []
        for slot_index in range(SLOTS):
            kernel_weight = kernels[chosen[slot_index]]
            masked = (slot_index < active_count).astype(jnp.float32)
            gate_scale = masked * gate_row[slot_index].astype(jnp.float32)
            pre = lax.optimization_barrier(convolve(window, kernel_weight).astype(jnp.bfloat16)).astype(jnp.float32)
            activated, slope = activation(pre)
            result = result + gate_scale * activated
            gate_terms.append(masked * jnp.sum(upstream * activated))
            grad_pre = (upstream * gate_scale * slope).astype(jnp.bfloat16)
            kernel_grad = kernel_grad.at[chosen[slot_index]].add(kernel_terms(window, grad_pre))
            rim_sum = rim_sum + lax.optimization_barrier(transpose_conv(grad_pre, kernel_weight).astype(jnp.bfloat16)).astype(jnp.float32)
        former = lax.dynamic_slice(grad_frame, (frame_index, first_row, anchor, anchor), (1, TILE_ROWS + 2, width, channels))
        grad_frame = lax.dynamic_update_slice(grad_frame, former + rim_sum[None], (frame_index, first_row, anchor, anchor))
        return (kernel_grad, grad_frame), (result.astype(jnp.bfloat16), jnp.stack(gate_terms))

    initial = (jnp.zeros((kernels.shape[0], 9, channels, channels), jnp.float32),
               jnp.zeros((frames.shape[0], frames.shape[1] + 2, width, channels), jnp.float32))
    position_list = jnp.arange(frames.shape[0] * N_TILE, dtype=jnp.int32)
    (kernel_grad, grad_frame), (tiles, gate_terms) = lax.scan(advance, initial, position_list)
    tiles = tiles.reshape(frames.shape[0], N_TILE, TILE_ROWS, width, channels)
    frames_out = tiles.reshape(frames.shape)
    input_grad = (cotangent.astype(jnp.float32) + grad_frame[:, 1:-1]).astype(jnp.bfloat16)
    gate_grad = gate_terms.reshape(frames.shape[0], N_TILE, SLOTS)
    return (frames_out, input_grad, gate_grad, kernel_grad)
```

```python
import functools

import jax
import jax.numpy as jnp
from jax import lax
from jax.experimental import pallas as pl
from jax.experimental.pallas import tpu as pltpu
from jax.sharding import PartitionSpec as P

CAP = 2


def shifts(columns, rows):
    place = lax.broadcasted_iota(jnp.int32, (rows, 1), 0) % columns

    def later(v):
        return jnp.where(place == 0, 0.0, pltpu.roll(v, 1, 0))

    def sooner(v):
        return jnp.where(place == columns - 1, 0.0, pltpu.roll(v, rows - 1, 0))

    return later, sooner


def owner_kernel(pick_ref, weight_ref, items_ref, bank_ref, back_ref, gate_ref, grad_ref):
    s = pl.program_id(0)
    cap, _, columns, channels = items_ref.shape[1:]
    rows = cap * columns
    later, sooner = shifts(columns, rows)

    @pl.when(s == 0)
    def _():
        grad_ref[...] = jnp.zeros_like(grad_ref)

    item = lax.broadcasted_iota(jnp.int32, (rows, 1), 0) // columns
    weight = jnp.zeros((rows, 1), jnp.float32)
    for c in range(cap):
        weight = jnp.where(item == c, weight_ref[s, c], weight)

    window = [items_ref[0, :, r].reshape(rows, channels) for r in range(3)]
    upstream = items_ref[0, :, 3].reshape(rows, channels).astype(jnp.float32)

    def column_term(db):
        total = jnp.dot(window[0], bank_ref[0, db], preferred_element_type=jnp.float32)
        for da in (1, 2):
            total = total + jnp.dot(
                window[da], bank_ref[0, 3 * da + db], preferred_element_type=jnp.float32
            )
        return total

    pre = column_term(1) + later(column_term(0)) + sooner(column_term(2))
    pre = pre.astype(jnp.bfloat16).astype(jnp.float32)
    squash = jax.nn.sigmoid(pre)
    activated = pre * squash
    slope = squash * (1.0 + pre * (1.0 - squash))
    back_ref[0, :, 3] = (weight * activated).astype(jnp.bfloat16).reshape(cap, columns, channels)
    gates = jnp.sum((upstream * activated).reshape(cap, columns, channels), axis=1)
    gate_ref[0] = jnp.broadcast_to(jnp.sum(gates, axis=1, keepdims=True), gate_ref.shape[1:])

    grad = (upstream * weight * slope).astype(jnp.bfloat16)
    for da in range(3):
        parts = [
            lax.dot_general(
                grad,
                bank_ref[0, 3 * da + db],
                (((1,), (1,)), ((), ())),
                preferred_element_type=jnp.float32,
            )
            for db in range(3)
        ]
        total = parts[1] + sooner(parts[0]) + later(parts[2])
        back_ref[0, :, da] = total.astype(jnp.bfloat16).reshape(cap, columns, channels)

    grad_wide = grad.astype(jnp.float32)
    moved = [sooner(grad_wide).astype(jnp.bfloat16), grad, later(grad_wide).astype(jnp.bfloat16)]
    e = pick_ref[s]
    chunks, _, _, share, _ = grad_ref.shape
    for db in range(3):
        for da in range(3):
            term = lax.dot_general(
                moved[db], window[da], (((0,), (0,)), ((), ())), preferred_element_type=jnp.float32
            )
            grad_ref[:, e, 3 * da + db] += term.reshape(chunks, share, channels)


def owner(pick, weight, items, kernels, chunks):
    sources, cap, _, columns, channels = items.shape
    experts, taps, _, outputs = kernels.shape
    spec = pltpu.PrefetchScalarGridSpec(
        num_scalar_prefetch=2,
        grid=(sources,),
        in_specs=[
            pl.BlockSpec((1, cap, 4, columns, channels), lambda s, p, w: (s, 0, 0, 0, 0)),
            pl.BlockSpec((1, taps, channels, outputs), lambda s, p, w: (p[s], 0, 0, 0)),
        ],
        out_specs=[
            pl.BlockSpec((1, cap, 4, columns, channels), lambda s, p, w: (s, 0, 0, 0, 0)),
            pl.BlockSpec((1, cap, 128), lambda s, p, w: (s, 0, 0)),
            pl.BlockSpec(
                (chunks, experts, taps, outputs // chunks, channels),
                lambda s, p, w: (0, 0, 0, 0, 0),
                pipeline_mode=pl.Buffered(1),
            ),
        ],
    )
    return pl.pallas_call(
        owner_kernel,
        grid_spec=spec,
        out_shape=[
            jax.ShapeDtypeStruct((sources, cap, 4, columns, channels), jnp.bfloat16),
            jax.ShapeDtypeStruct((sources, cap, 128), jnp.float32),
            jax.ShapeDtypeStruct(
                (chunks, experts, taps, outputs // chunks, channels), jnp.float32
            ),
        ],
        compiler_params=pltpu.CompilerParams(vmem_limit_bytes=48 * 1024 * 1024),
        name="owner",
    )(pick, weight, items, kernels)


def swap(x):
    return lax.all_to_all(x, "dp", split_axis=0, concat_axis=0, tiled=True)


def line(count):
    up = [(i, i + 1) for i in range(count - 1)]
    return up, [(j, i) for i, j in up]


def shards(frames, kernels, experts, counts, gate_weights, cotangent):
    owners = lax.axis_size("dp")
    tiles = lax.axis_size("tile")
    local = kernels.shape[0]
    up, down = line(tiles)
    before = lax.ppermute(frames[:, -1:], "tile", up)
    after = lax.ppermute(frames[:, :1], "tile", down)
    sheet = jnp.concatenate([before, frames, after, cotangent], axis=1)

    chosen = experts[:, 0]
    frame_count, slots = chosen.shape
    active = jnp.arange(slots)[None, :] < counts[:, 0][:, None]
    owner_of = chosen // local
    hit = (owner_of[:, :, None] == jnp.arange(owners)) & active[:, :, None]
    wanted = jnp.any(hit, axis=1)
    position = jnp.cumsum(wanted.astype(jnp.int32), axis=0) - 1
    slot_map = wanted.T[:, None, :] & (
        position.T[:, None, :] == jnp.arange(CAP)[None, :, None]
    )
    request = jnp.max(jnp.where(hit, (chosen % local)[:, :, None], 0), axis=(0, 1))
    tile_gate = jnp.sum(jnp.where(hit, gate_weights[:, 0][:, :, None], 0.0), axis=1)
    weight = jnp.sum(jnp.where(slot_map, tile_gate.T[:, None, :], 0.0), axis=2)
    note = jnp.concatenate([request[:, None].astype(jnp.float32), weight], axis=1)
    noted = swap(note)
    pick = noted[:, 0].astype(jnp.int32)
    shares = noted[:, 1:]

    picked = slot_map.astype(jnp.bfloat16).reshape(owners * CAP, frame_count)
    outgoing = jnp.dot(
        picked, sheet.reshape(frame_count, -1), preferred_element_type=jnp.float32
    ).astype(jnp.bfloat16)
    items = swap(outgoing.reshape((owners, CAP) + sheet.shape[1:]))

    back, gates, bank_grad = owner(pick, shares, items, kernels, tiles)
    kernel_part = lax.psum_scatter(bank_grad, "tile", scatter_dimension=0, tiled=True)[0]
    kernel_part = jnp.swapaxes(kernel_part, 2, 3)

    arrived = swap(back)
    gates = swap(gates[:, :, 0])
    selected = jnp.sum(jnp.where(slot_map, gates[:, :, None], 0.0), axis=1)
    gate_grad = jnp.sum(jnp.where(hit, selected.T[:, None, :], 0.0), axis=2)

    gathered = jnp.dot(
        picked.T, arrived.reshape(owners * CAP, -1), preferred_element_type=jnp.float32
    ).reshape(sheet.shape)
    result = (frames.astype(jnp.float32) + gathered[:, 3:4]).astype(jnp.bfloat16)
    from_above = lax.ppermute(gathered[:, 2:3].astype(jnp.bfloat16), "tile", up)
    from_below = lax.ppermute(gathered[:, 0:1].astype(jnp.bfloat16), "tile", down)
    input_grad = (
        cotangent.astype(jnp.float32)
        + gathered[:, 1:2]
        + from_above.astype(jnp.float32)
        + from_below.astype(jnp.float32)
    ).astype(jnp.bfloat16)
    return (result, input_grad, gate_grad[:, None, :], kernel_part)


def solution(mesh):
    return jax.shard_map(
        shards,
        mesh=mesh,
        in_specs=(
            P("dp", "tile", None, None),
            P("dp", None, None, None),
            P("dp", "tile", None),
            P("dp", "tile"),
            P("dp", "tile", None),
            P("dp", "tile", None, None),
        ),
        out_specs=(
            P("dp", "tile", None, None),
            P("dp", "tile", None, None),
            P("dp", "tile", None),
            P("dp", None, None, "tile"),
        ),
        check_vma=False,
    )
```

```python
import functools

import jax
import jax.numpy as jnp
from jax import lax
from jax.experimental import pallas as pl
from jax.experimental.pallas import tpu as pltpu
from jax.sharding import PartitionSpec as P

CAP = 2


def shifts(columns, rows):
    place = lax.broadcasted_iota(jnp.int32, (rows, 1), 0) % columns

    def later(v):
        return jnp.where(place == 0, 0.0, pltpu.roll(v, 1, 0))

    def sooner(v):
        return jnp.where(place == columns - 1, 0.0, pltpu.roll(v, rows - 1, 0))

    return later, sooner


def owner_kernel(
    pick_ref, weight_ref, place_ref, rim_ref,
    rows_ref, above_ref, below_ref, bank_ref, back_ref, gate_ref, grad_ref,
):
    s = pl.program_id(0)
    cap, _, columns, channels = back_ref.shape[1:]
    rows = cap * columns
    later, sooner = shifts(columns, rows)

    @pl.when(s == 0)
    def _():
        grad_ref[...] = jnp.zeros_like(grad_ref)

    item = lax.broadcasted_iota(jnp.int32, (rows, 1), 0) // columns
    weight = jnp.zeros((rows, 1), jnp.float32)
    for c in range(cap):
        weight = jnp.where(item == c, weight_ref[s, c], weight)

    def gather(ref, *lead):
        return jnp.concatenate([ref[(0,) + lead + (place_ref[s, c],)] for c in range(cap)], axis=0)

    blank = jnp.zeros((rows, channels), jnp.bfloat16)
    window = [
        jnp.where(rim_ref[0] > 0, gather(above_ref), blank),
        gather(rows_ref, 0),
        jnp.where(rim_ref[1] > 0, gather(below_ref), blank),
    ]
    upstream = gather(rows_ref, 1).astype(jnp.float32)

    def column_term(db):
        total = jnp.dot(window[0], bank_ref[0, db], preferred_element_type=jnp.float32)
        for da in (1, 2):
            total = total + jnp.dot(
                window[da], bank_ref[0, 3 * da + db], preferred_element_type=jnp.float32
            )
        return total

    pre = column_term(1) + later(column_term(0)) + sooner(column_term(2))
    pre = pre.astype(jnp.bfloat16).astype(jnp.float32)
    squash = jax.nn.sigmoid(pre)
    activated = pre * squash
    slope = squash * (1.0 + pre * (1.0 - squash))
    back_ref[0, :, 3] = (weight * activated).astype(jnp.bfloat16).reshape(cap, columns, channels)
    gates = jnp.sum((upstream * activated).reshape(cap, columns, channels), axis=1)
    gate_ref[0] = jnp.broadcast_to(jnp.sum(gates, axis=1, keepdims=True), gate_ref.shape[1:])

    grad = (upstream * weight * slope).astype(jnp.bfloat16)
    for da in range(3):
        parts = [
            lax.dot_general(
                grad,
                bank_ref[0, 3 * da + db],
                (((1,), (1,)), ((), ())),
                preferred_element_type=jnp.float32,
            )
            for db in range(3)
        ]
        total = parts[1] + sooner(parts[0]) + later(parts[2])
        back_ref[0, :, da] = total.astype(jnp.bfloat16).reshape(cap, columns, channels)

    grad_wide = grad.astype(jnp.float32)
    moved = [sooner(grad_wide).astype(jnp.bfloat16), grad, later(grad_wide).astype(jnp.bfloat16)]
    e = pick_ref[s]
    chunks, _, _, share, _ = grad_ref.shape
    for db in range(3):
        for da in range(3):
            term = lax.dot_general(
                moved[db], window[da], (((0,), (0,)), ((), ())), preferred_element_type=jnp.float32
            )
            grad_ref[:, e, 3 * da + db] += term.reshape(chunks, share, channels)


def owner(pick, weight, place, rim, rows, above, below, kernels, chunks):
    sources, _, frames, columns, channels = rows.shape
    experts, taps, _, outputs = kernels.shape
    spec = pltpu.PrefetchScalarGridSpec(
        num_scalar_prefetch=4,
        grid=(sources,),
        in_specs=[
            pl.BlockSpec((1, 2, frames, columns, channels), lambda s, *_: (s, 0, 0, 0, 0)),
            pl.BlockSpec((1, frames, columns, channels), lambda s, *_: (s, 0, 0, 0)),
            pl.BlockSpec((1, frames, columns, channels), lambda s, *_: (s, 0, 0, 0)),
            pl.BlockSpec((1, taps, channels, outputs), lambda s, p, *_: (p[s], 0, 0, 0)),
        ],
        out_specs=[
            pl.BlockSpec((1, CAP, 4, columns, channels), lambda s, *_: (s, 0, 0, 0, 0)),
            pl.BlockSpec((1, CAP, 128), lambda s, *_: (s, 0, 0)),
            pl.BlockSpec(
                (chunks, experts, taps, outputs // chunks, channels),
                lambda s, *_: (0, 0, 0, 0, 0),
                pipeline_mode=pl.Buffered(1),
            ),
        ],
    )
    return pl.pallas_call(
        owner_kernel,
        grid_spec=spec,
        out_shape=[
            jax.ShapeDtypeStruct((sources, CAP, 4, columns, channels), jnp.bfloat16),
            jax.ShapeDtypeStruct((sources, CAP, 128), jnp.float32),
            jax.ShapeDtypeStruct(
                (chunks, experts, taps, outputs // chunks, channels), jnp.float32
            ),
        ],
        compiler_params=pltpu.CompilerParams(vmem_limit_bytes=48 * 1024 * 1024),
        name="owner",
    )(pick, weight, place, rim, rows, above, below, kernels)


def grid_of(owners):
    across = 1
    while across * across * 4 <= owners:
        across *= 2
    while owners % across:
        across -= 1
    return owners // across, across


def remote(src, dst, send, recv, dp, tile):
    return pltpu.make_async_remote_copy(
        src_ref=src,
        dst_ref=dst,
        send_sem=send,
        recv_sem=recv,
        device_id=(dp, tile),
        device_id_type=pl.DeviceIdType.MESH,
    )


def spread_kernel(
    deep, across, tiles,
    own_ref, note_ref, rows_ref, above_ref, below_ref, noted_ref,
    local_sem, main_recv, above_recv, below_recv, note_recv,
    up_send, down_send, side_send, above_send, below_send, note_send,
):
    me, t = lax.axis_index("dp"), lax.axis_index("tile")
    z, x = me // across, me % across
    owners = deep * across
    has_above, has_below = t > 0, t < tiles - 1

    barrier = pltpu.get_barrier_semaphore()

    def greet(dp, tile):
        pl.semaphore_signal(
            barrier, inc=1, device_id=(dp, tile), device_id_type=pl.DeviceIdType.MESH
        )

    for j in range(1, owners):
        greet((me + j) % owners, t)
    pl.when(has_above)(lambda: greet(me, t - 1))
    pl.when(has_below)(lambda: greet(me, t + 1))
    pl.semaphore_wait(
        barrier, owners - 1 + has_above.astype(jnp.int32) + has_below.astype(jnp.int32)
    )

    started = []

    def launch(cond, make):
        if cond is None:
            make().start()
        else:
            pl.when(cond)(lambda: make().start())
        started.append((cond, make))

    def both(a, b):
        if a is None:
            return b
        return a if b is None else jnp.logical_and(a, b)

    def halos(cond, s, block):
        launch(
            both(cond, has_below),
            lambda: remote(block, above_ref.at[s], above_send.at[s], above_recv.at[s], me, t + 1),
        )
        launch(
            both(cond, has_above),
            lambda: remote(block, below_ref.at[s], below_send.at[s], below_recv.at[s], me, t - 1),
        )

    def lift(cond, s, block):
        launch(
            both(cond, z < deep - 1),
            lambda: remote(
                block, rows_ref.at[s], up_send.at[s], main_recv.at[s], me + across, t
            ),
        )

    def sink(cond, s, block):
        launch(
            both(cond, z > 0),
            lambda: remote(
                block, rows_ref.at[s], down_send.at[s], main_recv.at[s], me - across, t
            ),
        )

    def side(cond, s, block):
        for j in range(1, across):
            launch(
                cond,
                lambda j=j: remote(
                    block,
                    rows_ref.at[s],
                    side_send.at[j - 1, s],
                    main_recv.at[s],
                    z * across + (x + j) % across,
                    t,
                ),
            )

    def arrive(cond, s):
        def wait():
            remote(
                rows_ref.at[s], rows_ref.at[s], up_send.at[s], main_recv.at[s], me, t
            ).wait_recv()

        pl.when(cond)(wait) if cond is not None else wait()

    lift(None, me, own_ref)
    sink(None, me, own_ref)
    side(None, me, own_ref)
    halos(None, me, own_ref.at[0])
    for j in range(1, owners):
        peer = (me + j) % owners
        launch(
            None,
            lambda j=j, peer=peer: remote(
                note_ref.at[peer], noted_ref.at[me], note_send.at[j - 1], note_recv.at[me], peer, t
            ),
        )
    kept = pltpu.make_async_copy(own_ref, rows_ref.at[me], local_sem.at[0])
    kept.start()
    noted = pltpu.make_async_copy(note_ref.at[me], noted_ref.at[me], local_sem.at[1])
    noted.start()

    def side_arrivals(k):
        for sign in (1, -1) if k else (1,):
            zs = z - sign * k
            cond = (zs >= 0 if sign > 0 else zs < deep) if k else None
            for j in range(1, across):
                s = zs * across + (x + j) % across
                arrive(cond, s)
                halos(cond, s, rows_ref.at[s, 0])

    for k in range(1, deep):
        lower, upper = z - k, z + k
        s = lower * across + x
        arrive(lower >= 0, s)
        lift(lower >= 0, s, rows_ref.at[s])
        side(lower >= 0, s, rows_ref.at[s])
        halos(lower >= 0, s, rows_ref.at[s, 0])
        s = upper * across + x
        arrive(upper < deep, s)
        sink(upper < deep, s, rows_ref.at[s])
        side(upper < deep, s, rows_ref.at[s])
        halos(upper < deep, s, rows_ref.at[s, 0])
        side_arrivals(k - 1)
    side_arrivals(deep - 1)

    for j in range(1, owners):
        s = (me + j) % owners
        remote(
            note_ref.at[s], noted_ref.at[s], note_send.at[j - 1], note_recv.at[s], s, t
        ).wait_recv()
    for s in range(owners):
        pl.when(has_above)(
            lambda s=s: remote(
                above_ref.at[s], above_ref.at[s], above_send.at[s], above_recv.at[s], me, t
            ).wait_recv()
        )
        pl.when(has_below)(
            lambda s=s: remote(
                below_ref.at[s], below_ref.at[s], below_send.at[s], below_recv.at[s], me, t
            ).wait_recv()
        )
    for cond, make in started:
        if cond is None:
            make().wait_send()
        else:
            pl.when(cond)(lambda make=make: make().wait_send())
    kept.wait()
    noted.wait()


def spread(own, note, owners, tiles):
    deep, across = grid_of(owners)
    dma = pltpu.SemaphoreType.DMA
    anywhere = pl.BlockSpec(memory_space=pl.ANY)
    return pl.pallas_call(
        functools.partial(spread_kernel, deep, across, tiles),
        out_shape=[
            jax.ShapeDtypeStruct((owners,) + own.shape, own.dtype),
            jax.ShapeDtypeStruct((owners,) + own.shape[1:], own.dtype),
            jax.ShapeDtypeStruct((owners,) + own.shape[1:], own.dtype),
            jax.ShapeDtypeStruct(note.shape, note.dtype),
        ],
        in_specs=[pl.BlockSpec(memory_space=pltpu.VMEM)] * 2,
        out_specs=[anywhere] * 4,
        scratch_shapes=[
            dma((2,)), dma((owners,)), dma((owners,)), dma((owners,)), dma((owners,)),
            dma((owners,)), dma((owners,)), dma((max(across - 1, 1), owners)),
            dma((owners,)), dma((owners,)), dma((owners,)),
        ],
        compiler_params=pltpu.CompilerParams(
            collective_id=0, has_side_effects=True, vmem_limit_bytes=8 * 1024 * 1024
        ),
        name="spread",
    )(own, note)


def swap(x):
    return lax.all_to_all(x, "dp", split_axis=0, concat_axis=0, tiled=True)


def line(count):
    up = [(i, i + 1) for i in range(count - 1)]
    return up, [(j, i) for i, j in up]


def shards(frames, kernels, experts, counts, gate_weights, cotangent):
    owners = lax.axis_size("dp")
    tiles = lax.axis_size("tile")
    local = kernels.shape[0]
    up, down = line(tiles)
    chosen = experts[:, 0]
    frame_count, slots = chosen.shape
    active = jnp.arange(slots)[None, :] < counts[:, 0][:, None]
    owner_of = chosen // local
    hit = (owner_of[:, :, None] == jnp.arange(owners)) & active[:, :, None]
    wanted = jnp.any(hit, axis=1)
    position = jnp.cumsum(wanted.astype(jnp.int32), axis=0) - 1
    slot_map = wanted.T[:, None, :] & (
        position.T[:, None, :] == jnp.arange(CAP)[None, :, None]
    )
    request = jnp.max(jnp.where(hit, (chosen % local)[:, :, None], 0), axis=(0, 1))
    tile_gate = jnp.sum(jnp.where(hit, gate_weights[:, 0][:, :, None], 0.0), axis=1)
    weight = jnp.sum(jnp.where(slot_map, tile_gate.T[:, None, :], 0.0), axis=2)
    place = jnp.sum(
        jnp.where(slot_map, jnp.arange(frame_count)[None, None, :], 0), axis=2
    )
    note = jnp.concatenate(
        [request[:, None].astype(jnp.float32), weight, place.astype(jnp.float32)], axis=1
    )
    note = jnp.pad(note[:, None, :], ((0, 0), (0, 7), (0, 128 - note.shape[1])))
    own = jnp.stack([frames[:, 0], cotangent[:, 0]])
    rows, above, below, noted = spread(own, note, owners, tiles)
    noted = noted[:, 0]
    pick = noted[:, 0].astype(jnp.int32)
    shares = noted[:, 1 : 1 + CAP]
    places = noted[:, 1 + CAP : 1 + 2 * CAP].astype(jnp.int32)
    t = lax.axis_index("tile")
    rim = jnp.stack([t > 0, t < tiles - 1]).astype(jnp.int32)

    back, gates, bank_grad = owner(
        pick, shares, places, rim, rows, above, below, kernels, tiles
    )
    kernel_part = lax.psum_scatter(bank_grad, "tile", scatter_dimension=0, tiled=True)[0]
    kernel_part = jnp.swapaxes(kernel_part, 2, 3)

    arrived = swap(back)
    gates = swap(gates[:, :, 0])
    selected = jnp.sum(jnp.where(slot_map, gates[:, :, None], 0.0), axis=1)
    gate_grad = jnp.sum(jnp.where(hit, selected.T[:, None, :], 0.0), axis=2)

    picked = slot_map.astype(jnp.bfloat16).reshape(owners * CAP, frame_count)
    gathered = jnp.dot(
        picked.T, arrived.reshape(owners * CAP, -1), preferred_element_type=jnp.float32
    ).reshape((frame_count,) + arrived.shape[2:])
    result = (frames.astype(jnp.float32) + gathered[:, 3:4]).astype(jnp.bfloat16)
    from_above = lax.ppermute(gathered[:, 2:3].astype(jnp.bfloat16), "tile", up)
    from_below = lax.ppermute(gathered[:, 0:1].astype(jnp.bfloat16), "tile", down)
    input_grad = (
        cotangent.astype(jnp.float32)
        + gathered[:, 1:2]
        + from_above.astype(jnp.float32)
        + from_below.astype(jnp.float32)
    ).astype(jnp.bfloat16)
    return (result, input_grad, gate_grad[:, None, :], kernel_part)


def solution(mesh):
    return jax.shard_map(
        shards,
        mesh=mesh,
        in_specs=(
            P("dp", "tile", None, None),
            P("dp", None, None, None),
            P("dp", "tile", None),
            P("dp", "tile"),
            P("dp", "tile", None),
            P("dp", "tile", None, None),
        ),
        out_specs=(
            P("dp", "tile", None, None),
            P("dp", "tile", None, None),
            P("dp", "tile", None),
            P("dp", None, None, "tile"),
        ),
        check_vma=False,
    )
```

```python
import functools

import jax
import jax.numpy as jnp
from jax import lax
from jax.experimental import pallas as pl
from jax.experimental.pallas import tpu as pltpu
from jax.sharding import PartitionSpec as P

CAP = 2


def shifts(columns, rows):
    place = lax.broadcasted_iota(jnp.int32, (rows, 1), 0) % columns

    def later(v):
        return jnp.where(place == 0, 0.0, pltpu.roll(v, 1, 0))

    def sooner(v):
        return jnp.where(place == columns - 1, 0.0, pltpu.roll(v, rows - 1, 0))

    return later, sooner


def owner_kernel(
    pick_ref, weight_ref, place_ref, rim_ref,
    rows_ref, above_ref, below_ref, bank_ref, back_ref, gate_ref, out_ref, grad_ref,
):
    s = pl.program_id(0)
    cap = CAP
    columns, channels = back_ref.shape[3:]
    steps = out_ref.shape[1]
    rows = cap * columns
    later, sooner = shifts(columns, rows)

    @pl.when(s == 0)
    def _():
        @pl.loop(0, steps)
        def _(i):
            grad_ref[:, i] = jnp.zeros_like(grad_ref[:, i])

    back_ref[...] = jnp.zeros_like(back_ref)

    item = lax.broadcasted_iota(jnp.int32, (rows, 1), 0) // columns
    weight = jnp.zeros((rows, 1), jnp.float32)
    for c in range(cap):
        weight = jnp.where(item == c, weight_ref[s, c], weight)

    def gather(ref, *lead):
        return jnp.concatenate([ref[(0,) + lead + (place_ref[s, c],)] for c in range(cap)], axis=0)

    blank = jnp.zeros((rows, channels), jnp.bfloat16)
    window = [
        jnp.where(rim_ref[0] > 0, gather(above_ref), blank),
        gather(rows_ref, 0),
        jnp.where(rim_ref[1] > 0, gather(below_ref), blank),
    ]
    upstream = gather(rows_ref, 1).astype(jnp.float32)

    def column_term(db):
        total = jnp.dot(window[0], bank_ref[0, db], preferred_element_type=jnp.float32)
        for da in (1, 2):
            total = total + jnp.dot(
                window[da], bank_ref[0, 3 * da + db], preferred_element_type=jnp.float32
            )
        return total

    pre = column_term(1) + later(column_term(0)) + sooner(column_term(2))
    pre = pre.astype(jnp.bfloat16).astype(jnp.float32)
    squash = jax.nn.sigmoid(pre)
    activated = pre * squash
    slope = squash * (1.0 + pre * (1.0 - squash))

    def put(r, value):
        value = value.astype(jnp.bfloat16).reshape(cap, columns, channels)
        for c in reversed(range(cap)):
            back_ref[0, r, place_ref[s, c]] = value[c]

    put(3, weight * activated)
    gates = jnp.sum((upstream * activated).reshape(cap, columns, channels), axis=1)
    gates = jnp.broadcast_to(jnp.sum(gates, axis=1, keepdims=True), (cap, 128))
    gate_ref[0] = jnp.concatenate([gates, jnp.zeros((8 - cap, 128), jnp.float32)], axis=0)

    grad = (upstream * weight * slope).astype(jnp.bfloat16)
    for da in range(3):
        parts = [
            lax.dot_general(
                grad,
                bank_ref[0, 3 * da + db],
                (((1,), (1,)), ((), ())),
                preferred_element_type=jnp.float32,
            )
            for db in range(3)
        ]
        total = parts[1] + sooner(parts[0]) + later(parts[2])
        put(da, total)

    grad_wide = grad.astype(jnp.float32)
    moved = [sooner(grad_wide).astype(jnp.bfloat16), grad, later(grad_wide).astype(jnp.bfloat16)]
    e = pick_ref[s]
    chunks, _, share, _ = grad_ref.shape
    taps = bank_ref.shape[1]
    for db in range(3):
        for da in range(3):
            term = lax.dot_general(
                moved[db], window[da], (((0,), (0,)), ((), ())), preferred_element_type=jnp.float32
            )
            grad_ref[:, e * taps + 3 * da + db] += term.reshape(chunks, share, channels)

    @pl.when(s == pl.num_programs(0) - 1)
    def _():
        @pl.loop(0, steps)
        def _(i):
            out_ref[:, i] = grad_ref[:, i].astype(out_ref.dtype)


def owner(pick, weight, place, rim, rows, above, below, kernels, chunks):
    sources, _, frames, columns, channels = rows.shape
    experts, taps, _, outputs = kernels.shape
    spec = pltpu.PrefetchScalarGridSpec(
        num_scalar_prefetch=4,
        grid=(sources,),
        in_specs=[
            pl.BlockSpec((1, 2, frames, columns, channels), lambda s, *_: (s, 0, 0, 0, 0)),
            pl.BlockSpec((1, frames, columns, channels), lambda s, *_: (s, 0, 0, 0)),
            pl.BlockSpec((1, frames, columns, channels), lambda s, *_: (s, 0, 0, 0)),
            pl.BlockSpec((1, taps, channels, outputs), lambda s, p, *_: (p[s], 0, 0, 0)),
        ],
        out_specs=[
            pl.BlockSpec((1, 4, frames, columns, channels), lambda s, *_: (s, 0, 0, 0, 0)),
            pl.BlockSpec((1, 8, 128), lambda s, *_: (s, 0, 0)),
            pl.BlockSpec(
                (chunks, experts * taps, outputs // chunks, channels),
                lambda s, *_: (0, 0, 0, 0),
                pipeline_mode=pl.Buffered(1),
            ),
        ],
        scratch_shapes=[
            pltpu.VMEM((chunks, experts * taps, outputs // chunks, channels), jnp.float32)
        ],
    )
    return pl.pallas_call(
        owner_kernel,
        grid_spec=spec,
        out_shape=[
            jax.ShapeDtypeStruct((sources, 4, frames, columns, channels), jnp.bfloat16),
            jax.ShapeDtypeStruct((sources, 8, 128), jnp.float32),
            jax.ShapeDtypeStruct(
                (chunks, experts * taps, outputs // chunks, channels), jnp.bfloat16
            ),
        ],
        compiler_params=pltpu.CompilerParams(vmem_limit_bytes=48 * 1024 * 1024),
        name="owner",
    )(pick, weight, place, rim, rows, above, below, kernels)


def grid_of(owners):
    across = 1
    while across * across * 4 <= owners:
        across *= 2
    while owners % across:
        across -= 1
    return owners // across, across


def remote(src, dst, send, recv, dp, tile):
    return pltpu.make_async_remote_copy(
        src_ref=src,
        dst_ref=dst,
        send_sem=send,
        recv_sem=recv,
        device_id=(dp, tile),
        device_id_type=pl.DeviceIdType.MESH,
    )


def spread_kernel(
    deep, across, tiles,
    own_ref, note_ref, rows_ref, above_ref, below_ref, noted_ref,
    local_sem, main_recv, above_recv, below_recv, note_recv,
    up_send, down_send, side_send, above_send, below_send, note_send,
):
    me, t = lax.axis_index("dp"), lax.axis_index("tile")
    z, x = me // across, me % across
    owners = deep * across
    has_above, has_below = t > 0, t < tiles - 1

    barrier = pltpu.get_barrier_semaphore()

    def greet(dp, tile):
        pl.semaphore_signal(
            barrier, inc=1, device_id=(dp, tile), device_id_type=pl.DeviceIdType.MESH
        )

    for j in range(1, owners):
        greet((me + j) % owners, t)
    pl.when(has_above)(lambda: greet(me, t - 1))
    pl.when(has_below)(lambda: greet(me, t + 1))
    pl.semaphore_wait(
        barrier, owners - 1 + has_above.astype(jnp.int32) + has_below.astype(jnp.int32)
    )

    started = []

    def launch(cond, make):
        if cond is None:
            make().start()
        else:
            pl.when(cond)(lambda: make().start())
        started.append((cond, make))

    def both(a, b):
        if a is None:
            return b
        return a if b is None else jnp.logical_and(a, b)

    def halos(cond, s, block):
        launch(
            both(cond, has_below),
            lambda: remote(block, above_ref.at[s], above_send.at[s], above_recv.at[s], me, t + 1),
        )
        launch(
            both(cond, has_above),
            lambda: remote(block, below_ref.at[s], below_send.at[s], below_recv.at[s], me, t - 1),
        )

    def lift(cond, s, block):
        launch(
            both(cond, z < deep - 1),
            lambda: remote(
                block, rows_ref.at[s], up_send.at[s], main_recv.at[s], me + across, t
            ),
        )

    def sink(cond, s, block):
        launch(
            both(cond, z > 0),
            lambda: remote(
                block, rows_ref.at[s], down_send.at[s], main_recv.at[s], me - across, t
            ),
        )

    def side(cond, s, block):
        for j in range(1, across):
            launch(
                cond,
                lambda j=j: remote(
                    block,
                    rows_ref.at[s],
                    side_send.at[j - 1, s],
                    main_recv.at[s],
                    z * across + (x + j) % across,
                    t,
                ),
            )

    def arrive(cond, s):
        def wait():
            remote(
                rows_ref.at[s], rows_ref.at[s], up_send.at[s], main_recv.at[s], me, t
            ).wait_recv()

        pl.when(cond)(wait) if cond is not None else wait()

    lift(None, me, own_ref)
    sink(None, me, own_ref)
    side(None, me, own_ref)
    halos(None, me, own_ref.at[0])
    for j in range(1, owners):
        peer = (me + j) % owners
        launch(
            None,
            lambda j=j, peer=peer: remote(
                note_ref.at[peer], noted_ref.at[me], note_send.at[j - 1], note_recv.at[me], peer, t
            ),
        )
    kept = pltpu.make_async_copy(own_ref, rows_ref.at[me], local_sem.at[0])
    kept.start()
    noted = pltpu.make_async_copy(note_ref.at[me], noted_ref.at[me], local_sem.at[1])
    noted.start()

    def side_arrivals(k):
        for sign in (1, -1) if k else (1,):
            zs = z - sign * k
            cond = (zs >= 0 if sign > 0 else zs < deep) if k else None
            for j in range(1, across):
                s = zs * across + (x + j) % across
                arrive(cond, s)
                halos(cond, s, rows_ref.at[s, 0])

    for k in range(1, deep):
        lower, upper = z - k, z + k
        s = lower * across + x
        arrive(lower >= 0, s)
        lift(lower >= 0, s, rows_ref.at[s])
        side(lower >= 0, s, rows_ref.at[s])
        halos(lower >= 0, s, rows_ref.at[s, 0])
        s = upper * across + x
        arrive(upper < deep, s)
        sink(upper < deep, s, rows_ref.at[s])
        side(upper < deep, s, rows_ref.at[s])
        halos(upper < deep, s, rows_ref.at[s, 0])
        side_arrivals(k - 1)
    side_arrivals(deep - 1)

    for j in range(1, owners):
        s = (me + j) % owners
        remote(
            note_ref.at[s], noted_ref.at[s], note_send.at[j - 1], note_recv.at[s], s, t
        ).wait_recv()
    for s in range(owners):
        pl.when(has_above)(
            lambda s=s: remote(
                above_ref.at[s], above_ref.at[s], above_send.at[s], above_recv.at[s], me, t
            ).wait_recv()
        )
        pl.when(has_below)(
            lambda s=s: remote(
                below_ref.at[s], below_ref.at[s], below_send.at[s], below_recv.at[s], me, t
            ).wait_recv()
        )
    for cond, make in started:
        if cond is None:
            make().wait_send()
        else:
            pl.when(cond)(lambda make=make: make().wait_send())
    kept.wait()
    noted.wait()


def spread(own, note, owners, tiles):
    deep, across = grid_of(owners)
    dma = pltpu.SemaphoreType.DMA
    anywhere = pl.BlockSpec(memory_space=pl.ANY)
    return pl.pallas_call(
        functools.partial(spread_kernel, deep, across, tiles),
        out_shape=[
            jax.ShapeDtypeStruct((owners,) + own.shape, own.dtype),
            jax.ShapeDtypeStruct((owners,) + own.shape[1:], own.dtype),
            jax.ShapeDtypeStruct((owners,) + own.shape[1:], own.dtype),
            jax.ShapeDtypeStruct(note.shape, note.dtype),
        ],
        in_specs=[pl.BlockSpec(memory_space=pltpu.VMEM)] * 2,
        out_specs=[anywhere] * 4,
        scratch_shapes=[
            dma((2,)), dma((owners,)), dma((owners,)), dma((owners,)), dma((owners,)),
            dma((owners,)), dma((owners,)), dma((max(across - 1, 1), owners)),
            dma((owners,)), dma((owners,)), dma((owners,)),
        ],
        compiler_params=pltpu.CompilerParams(
            collective_id=0, has_side_effects=True, vmem_limit_bytes=8 * 1024 * 1024
        ),
        name="spread",
    )(own, note)


def collect_kernel(
    deep, across, high, cores,
    terms_ref, gate_ref, bank_ref, own_ref,
    result_ref, input_ref, gated_ref, grad_ref,
    above, below, side_out, side_in, far_out, far_in, total, mate_in, band_out, band_in,
    local_sem, above_send, above_recv, below_send, below_recv,
    side_send, side_recv, far_send, far_recv, mate_send, mate_recv, band_send, band_recv,
    gate_send, gate_recv,
):
    me, t = lax.axis_index("dp"), lax.axis_index("tile")
    z, x = me // across, me % across
    y, core = t // cores, t % cores
    owners, tiles = deep * across, high * cores
    frames = own_ref.shape[1]
    steps = grad_ref.shape[0]
    has_above, has_below = t > 0, t < tiles - 1

    barrier = pltpu.get_barrier_semaphore()
    for j in range(1, owners):
        pl.semaphore_signal(
            barrier, device_id=((me + j) % owners, t), device_id_type=pl.DeviceIdType.MESH
        )
    for j in range(1, tiles):
        pl.semaphore_signal(
            barrier, device_id=(me, (t + j) % tiles), device_id_type=pl.DeviceIdType.MESH
        )
    pl.semaphore_wait(barrier, owners - 1 + tiles - 1)

    started = []

    def launch(make, cond=None):
        if cond is None:
            make().start()
        else:
            pl.when(cond)(lambda: make().start())
        started.append((cond, make))

    ring = [(z + k) % deep for k in list(range(1, deep)) + [0]]

    def lower(s):
        return remote(terms_ref.at[s, 2], above.at[s], above_send.at[s], above_recv.at[s], me, t + 1)

    def upper(s):
        return remote(terms_ref.at[s, 0], below.at[s], below_send.at[s], below_recv.at[s], me, t - 1)

    for j in list(range(1, across)) + [0]:
        for zs in ring:
            s = zs * across + (x + j) % across
            launch(lambda s=s: lower(s), has_below)
            launch(lambda s=s: upper(s), has_above)

    bands = [(y + k) % high for k in list(range(1, high)) + [0]]
    for k, ys in enumerate(bands):
        for j in range(1, cores):
            mate = (core + j) % cores
            launch(
                lambda k=k, j=j, ys=ys, mate=mate: remote(
                    bank_ref.at[ys * cores + mate],
                    mate_in.at[k, j - 1],
                    mate_send.at[k, j - 1],
                    mate_recv.at[k, j - 1],
                    me,
                    y * cores + mate,
                )
            )
    for j in range(1, owners):
        peer = (me + j) % owners
        launch(
            lambda j=j, peer=peer: remote(
                gate_ref.at[peer], gated_ref.at[me], gate_send.at[j - 1], gate_recv.at[j - 1], peer, t
            )
        )
    kept = pltpu.make_async_copy(gate_ref.at[me], gated_ref.at[me], local_sem.at[0])
    kept.start()

    @pl.when(jnp.logical_not(has_above))
    def _():
        above[...] = jnp.zeros_like(above)

    @pl.when(jnp.logical_not(has_below))
    def _():
        below[...] = jnp.zeros_like(below)

    def rims(s):
        pl.when(has_above)(
            lambda: remote(
                above.at[s], above.at[s], above_send.at[s], above_recv.at[s], me, t - 1
            ).wait_recv()
        )
        pl.when(has_below)(
            lambda: remote(
                below.at[s], below.at[s], below_send.at[s], below_recv.at[s], me, t + 1
            ).wait_recv()
        )

    def wide(ref, *at):
        return ref[at].astype(jnp.float32)

    def row(s, f):
        return wide(terms_ref, s, 1, f) + wide(above, s, f) + wide(below, s, f)

    for k, zs in enumerate(ring):
        for j in range(1, across):
            xs = (x + j) % across
            s = zs * across + xs
            rims(s)

            @pl.loop(0, frames)
            def _(f):
                side_out[j - 1, k, 0, f] = row(s, f).astype(jnp.bfloat16)
                side_out[j - 1, k, 1, f] = terms_ref[s, 3, f]

            launch(
                lambda k=k, j=j, xs=xs: remote(
                    side_out.at[j - 1, k],
                    side_in.at[j - 1, k],
                    side_send.at[j - 1, k],
                    side_recv.at[j - 1, k],
                    z * across + xs,
                    t,
                )
            )

    for k, ys in enumerate(bands):
        for j in range(1, cores):
            remote(
                mate_in.at[k, j - 1], mate_in.at[k, j - 1],
                mate_send.at[k, j - 1], mate_recv.at[k, j - 1],
                me, y * cores + (core + j) % cores,
            ).wait_recv()
        if k < high - 1:

            @pl.loop(0, steps)
            def _(i):
                value = wide(bank_ref, ys * cores + core, i)
                for j in range(1, cores):
                    value = value + wide(mate_in, k, j - 1, i)
                band_out[k, i] = value.astype(jnp.bfloat16)

            launch(
                lambda k=k, ys=ys: remote(
                    band_out.at[k], band_in.at[k], band_send.at[k], band_recv.at[k],
                    me, ys * cores + core,
                )
            )

    for k, zs in enumerate(ring):
        s = zs * across + x
        rims(s)
        for j in range(1, across):
            remote(
                side_in.at[j - 1, k], side_in.at[j - 1, k],
                side_send.at[j - 1, k], side_recv.at[j - 1, k],
                z * across + (x + j) % across, t,
            ).wait_recv()

        def summed(f):
            first, second = row(s, f), wide(terms_ref, s, 3, f)
            for j in range(1, across):
                first = first + wide(side_in, j - 1, k, 0, f)
                second = second + wide(side_in, j - 1, k, 1, f)
            return first, second

        if k < deep - 1:

            @pl.loop(0, frames)
            def _(f):
                first, second = summed(f)
                far_out[k, 0, f] = first.astype(jnp.bfloat16)
                far_out[k, 1, f] = second.astype(jnp.bfloat16)

            launch(
                lambda k=k, zs=zs: remote(
                    far_out.at[k], far_in.at[k], far_send.at[k], far_recv.at[k],
                    zs * across + x, t,
                )
            )
        else:

            @pl.loop(0, frames)
            def _(f):
                first, second = summed(f)
                total[0, f] = wide(own_ref, 1, f) + first
                total[1, f] = wide(own_ref, 0, f) + second

    for k in range(high - 1):
        remote(
            band_in.at[k], band_in.at[k], band_send.at[k], band_recv.at[k],
            me, bands[k] * cores + core,
        ).wait_recv()

    @pl.loop(0, steps)
    def _(i):
        value = wide(bank_ref, t, i)
        for j in range(1, cores):
            value = value + wide(mate_in, high - 1, j - 1, i)
        for k in range(high - 1):
            value = value + wide(band_in, k, i)
        grad_ref[i] = value

    for k in range(deep - 1):
        remote(
            far_in.at[k], far_in.at[k], far_send.at[k], far_recv.at[k], ring[k] * across + x, t
        ).wait_recv()

    @pl.loop(0, frames)
    def _(f):
        first, second = total[0, f], total[1, f]
        for k in range(deep - 1):
            first = first + wide(far_in, k, 0, f)
            second = second + wide(far_in, k, 1, f)
        input_ref[f] = first.astype(jnp.bfloat16)
        result_ref[f] = second.astype(jnp.bfloat16)

    for j in range(1, owners):
        s = (me + owners - j) % owners
        remote(
            gate_ref.at[s], gated_ref.at[s], gate_send.at[j - 1], gate_recv.at[j - 1], s, t
        ).wait_recv()
    for cond, make in started:
        if cond is None:
            make().wait_send()
        else:
            pl.when(cond)(lambda make=make: make().wait_send())
    kept.wait()


def collect(terms, gates, bank, own):
    owners, _, frames, columns, channels = terms.shape
    tiles, steps, share, _ = bank.shape
    deep, across = grid_of(owners)
    cores = 1 if tiles % 2 else 2
    high = tiles // cores
    dma = pltpu.SemaphoreType.DMA
    vmem = pl.BlockSpec(memory_space=pltpu.VMEM)
    beside, past, mates, far = (max(v - 1, 1) for v in (across, deep, cores, high))
    block = (2, frames, columns, channels)

    def room(*shape):
        return pltpu.VMEM(shape, jnp.bfloat16)

    return pl.pallas_call(
        functools.partial(collect_kernel, deep, across, high, cores),
        out_shape=[
            jax.ShapeDtypeStruct(block[1:], jnp.bfloat16),
            jax.ShapeDtypeStruct(block[1:], jnp.bfloat16),
            jax.ShapeDtypeStruct(gates.shape, gates.dtype),
            jax.ShapeDtypeStruct(bank.shape[1:], jnp.float32),
        ],
        in_specs=[vmem] * 4,
        out_specs=[vmem] * 4,
        scratch_shapes=[
            room(owners, *block[1:]),
            room(owners, *block[1:]),
            room(beside, deep, *block),
            room(beside, deep, *block),
            room(past, *block),
            room(past, *block),
            pltpu.VMEM(block, jnp.float32),
            room(high, mates, steps, share, channels),
            room(far, steps, share, channels),
            room(far, steps, share, channels),
            dma((1,)),
            dma((owners,)), dma((owners,)), dma((owners,)), dma((owners,)),
            dma((beside, deep)), dma((beside, deep)),
            dma((past,)), dma((past,)),
            dma((high, mates)), dma((high, mates)),
            dma((far,)), dma((far,)),
            dma((max(owners - 1, 1),)), dma((max(owners - 1, 1),)),
        ],
        compiler_params=pltpu.CompilerParams(
            collective_id=1, has_side_effects=True, vmem_limit_bytes=56 * 1024 * 1024
        ),
        name="collect",
    )(terms, gates, bank, own)


def shards(frames, kernels, experts, counts, gate_weights, cotangent):
    owners = lax.axis_size("dp")
    tiles = lax.axis_size("tile")
    local = kernels.shape[0]
    chosen = experts[:, 0]
    frame_count, slots = chosen.shape
    active = jnp.arange(slots)[None, :] < counts[:, 0][:, None]
    owner_of = chosen // local
    hit = (owner_of[:, :, None] == jnp.arange(owners)) & active[:, :, None]
    wanted = jnp.any(hit, axis=1)
    position = jnp.cumsum(wanted.astype(jnp.int32), axis=0) - 1
    slot_map = wanted.T[:, None, :] & (
        position.T[:, None, :] == jnp.arange(CAP)[None, :, None]
    )
    request = jnp.max(jnp.where(hit, (chosen % local)[:, :, None], 0), axis=(0, 1))
    tile_gate = jnp.sum(jnp.where(hit, gate_weights[:, 0][:, :, None], 0.0), axis=1)
    weight = jnp.sum(jnp.where(slot_map, tile_gate.T[:, None, :], 0.0), axis=2)
    place = jnp.sum(
        jnp.where(slot_map, jnp.arange(frame_count)[None, None, :], 0), axis=2
    )
    note = jnp.concatenate(
        [request[:, None].astype(jnp.float32), weight, place.astype(jnp.float32)], axis=1
    )
    note = jnp.pad(note[:, None, :], ((0, 0), (0, 7), (0, 128 - note.shape[1])))
    own = jnp.stack([frames[:, 0], cotangent[:, 0]])
    rows, above, below, noted = spread(own, note, owners, tiles)
    noted = noted[:, 0]
    pick = noted[:, 0].astype(jnp.int32)
    shares = noted[:, 1 : 1 + CAP]
    places = noted[:, 1 + CAP : 1 + 2 * CAP].astype(jnp.int32)
    t = lax.axis_index("tile")
    rim = jnp.stack([t > 0, t < tiles - 1]).astype(jnp.int32)

    back, gates, bank_grad = owner(
        pick, shares, places, rim, rows, above, below, kernels, tiles
    )
    result, input_grad, gated, bank_part = collect(back, gates, bank_grad, own)
    kernel_part = jnp.swapaxes(bank_part, 1, 2).reshape(
        kernels.shape[:3] + (bank_part.shape[1],)
    )
    gated = gated[:, :CAP, 0]
    selected = jnp.sum(jnp.where(slot_map, gated[:, :, None], 0.0), axis=1)
    gate_grad = jnp.sum(jnp.where(hit, selected.T[:, None, :], 0.0), axis=2)
    return (result[:, None], input_grad[:, None], gate_grad[:, None, :], kernel_part)


def solution(mesh):
    return jax.shard_map(
        shards,
        mesh=mesh,
        in_specs=(
            P("dp", "tile", None, None),
            P("dp", None, None, None),
            P("dp", "tile", None),
            P("dp", "tile"),
            P("dp", "tile", None),
            P("dp", "tile", None, None),
        ),
        out_specs=(
            P("dp", "tile", None, None),
            P("dp", "tile", None, None),
            P("dp", "tile", None),
            P("dp", None, None, "tile"),
        ),
        check_vma=False,
    )
```

```python
import functools

import jax
import jax.numpy as jnp
from jax import lax
from jax.experimental import pallas as pl
from jax.experimental.pallas import tpu as pltpu
from jax.sharding import PartitionSpec as P

CAP = 2


def shifts(columns, rows):
    place = lax.broadcasted_iota(jnp.int32, (rows, 1), 0) % columns

    def later(v):
        return jnp.where(place == 0, 0.0, pltpu.roll(v, 1, 0))

    def sooner(v):
        return jnp.where(place == columns - 1, 0.0, pltpu.roll(v, rows - 1, 0))

    return later, sooner


def owner_kernel(
    pick_ref, weight_ref, place_ref, rim_ref,
    rows_ref, above_ref, below_ref, bank_ref, back_ref, gate_ref, out_ref, grad_ref,
):
    s = pl.program_id(0)
    cap = CAP
    columns, channels = back_ref.shape[3:]
    steps = out_ref.shape[1]
    rows = cap * columns
    later, sooner = shifts(columns, rows)

    @pl.when(s == 0)
    def _():
        @pl.loop(0, steps)
        def _(i):
            grad_ref[:, i] = jnp.zeros_like(grad_ref[:, i])

    back_ref[...] = jnp.zeros_like(back_ref)

    item = lax.broadcasted_iota(jnp.int32, (rows, 1), 0) // columns
    weight = jnp.zeros((rows, 1), jnp.float32)
    for c in range(cap):
        weight = jnp.where(item == c, weight_ref[s, c], weight)

    def gather(ref, *lead):
        return jnp.concatenate([ref[(0,) + lead + (place_ref[s, c],)] for c in range(cap)], axis=0)

    blank = jnp.zeros((rows, channels), jnp.bfloat16)
    window = [
        jnp.where(rim_ref[0] > 0, gather(above_ref), blank),
        gather(rows_ref, 0),
        jnp.where(rim_ref[1] > 0, gather(below_ref), blank),
    ]
    upstream = gather(rows_ref, 1).astype(jnp.float32)

    def column_term(db):
        total = jnp.dot(window[0], bank_ref[0, db], preferred_element_type=jnp.float32)
        for da in (1, 2):
            total = total + jnp.dot(
                window[da], bank_ref[0, 3 * da + db], preferred_element_type=jnp.float32
            )
        return total

    pre = column_term(1) + later(column_term(0)) + sooner(column_term(2))
    pre = pre.astype(jnp.bfloat16).astype(jnp.float32)
    squash = jax.nn.sigmoid(pre)
    activated = pre * squash
    slope = squash * (1.0 + pre * (1.0 - squash))

    def put(r, value):
        value = value.astype(jnp.bfloat16).reshape(cap, columns, channels)
        for c in reversed(range(cap)):
            back_ref[0, r, place_ref[s, c]] = value[c]

    put(3, weight * activated)
    gates = jnp.sum((upstream * activated).reshape(cap, columns, channels), axis=1)
    gates = jnp.broadcast_to(jnp.sum(gates, axis=1, keepdims=True), (cap, 128))
    gate_ref[0] = jnp.concatenate([gates, jnp.zeros((8 - cap, 128), jnp.float32)], axis=0)

    grad = (upstream * weight * slope).astype(jnp.bfloat16)
    for da in range(3):
        parts = [
            lax.dot_general(
                grad,
                bank_ref[0, 3 * da + db],
                (((1,), (1,)), ((), ())),
                preferred_element_type=jnp.float32,
            )
            for db in range(3)
        ]
        total = parts[1] + sooner(parts[0]) + later(parts[2])
        put(da, total)

    grad_wide = grad.astype(jnp.float32)
    moved = [sooner(grad_wide).astype(jnp.bfloat16), grad, later(grad_wide).astype(jnp.bfloat16)]
    e = pick_ref[s]
    chunks, _, share, _ = grad_ref.shape
    taps = bank_ref.shape[1]
    for db in range(3):
        for da in range(3):
            term = lax.dot_general(
                moved[db], window[da], (((0,), (0,)), ((), ())), preferred_element_type=jnp.float32
            )
            grad_ref[:, e * taps + 3 * da + db] += term.reshape(chunks, share, channels)

    @pl.when(s == pl.num_programs(0) - 1)
    def _():
        @pl.loop(0, steps)
        def _(i):
            out_ref[:, i] = grad_ref[:, i].astype(out_ref.dtype)


def owner(pick, weight, place, rim, rows, above, below, kernels, chunks):
    sources, _, frames, columns, channels = rows.shape
    experts, taps, _, outputs = kernels.shape
    spec = pltpu.PrefetchScalarGridSpec(
        num_scalar_prefetch=4,
        grid=(sources,),
        in_specs=[
            pl.BlockSpec((1, 2, frames, columns, channels), lambda s, *_: (s, 0, 0, 0, 0)),
            pl.BlockSpec((1, frames, columns, channels), lambda s, *_: (s, 0, 0, 0)),
            pl.BlockSpec((1, frames, columns, channels), lambda s, *_: (s, 0, 0, 0)),
            pl.BlockSpec((1, taps, channels, outputs), lambda s, p, *_: (p[s], 0, 0, 0)),
        ],
        out_specs=[
            pl.BlockSpec((1, 4, frames, columns, channels), lambda s, *_: (s, 0, 0, 0, 0)),
            pl.BlockSpec((1, 8, 128), lambda s, *_: (s, 0, 0)),
            pl.BlockSpec(
                (chunks, experts * taps, outputs // chunks, channels),
                lambda s, *_: (0, 0, 0, 0),
                pipeline_mode=pl.Buffered(1),
            ),
        ],
        scratch_shapes=[
            pltpu.VMEM((chunks, experts * taps, outputs // chunks, channels), jnp.float32)
        ],
    )
    return pl.pallas_call(
        owner_kernel,
        grid_spec=spec,
        out_shape=[
            jax.ShapeDtypeStruct((sources, 4, frames, columns, channels), jnp.bfloat16),
            jax.ShapeDtypeStruct((sources, 8, 128), jnp.float32),
            jax.ShapeDtypeStruct(
                (chunks, experts * taps, outputs // chunks, channels), jnp.bfloat16
            ),
        ],
        compiler_params=pltpu.CompilerParams(vmem_limit_bytes=48 * 1024 * 1024),
        name="owner",
    )(pick, weight, place, rim, rows, above, below, kernels)


def grid_of(owners):
    across = 1
    while across * across * 4 <= owners:
        across *= 2
    while owners % across:
        across -= 1
    return owners // across, across


def remote(src, dst, send, recv, dp, tile):
    return pltpu.make_async_remote_copy(
        src_ref=src,
        dst_ref=dst,
        send_sem=send,
        recv_sem=recv,
        device_id=(dp, tile),
        device_id_type=pl.DeviceIdType.MESH,
    )


def spread_kernel(
    deep, across, tiles,
    own_ref, note_ref, rows_ref, above_ref, below_ref, noted_ref,
    local_sem, main_recv, above_recv, below_recv, note_recv,
    up_send, down_send, side_send, above_send, below_send, note_send,
):
    me, t = lax.axis_index("dp"), lax.axis_index("tile")
    z, x = me // across, me % across
    owners = deep * across
    has_above, has_below = t > 0, t < tiles - 1

    barrier = pltpu.get_barrier_semaphore()

    def greet(dp, tile):
        pl.semaphore_signal(
            barrier, inc=1, device_id=(dp, tile), device_id_type=pl.DeviceIdType.MESH
        )

    for j in range(1, owners):
        greet((me + j) % owners, t)
    pl.when(has_above)(lambda: greet(me, t - 1))
    pl.when(has_below)(lambda: greet(me, t + 1))
    pl.semaphore_wait(
        barrier, owners - 1 + has_above.astype(jnp.int32) + has_below.astype(jnp.int32)
    )

    started = []

    def launch(cond, make):
        if cond is None:
            make().start()
        else:
            pl.when(cond)(lambda: make().start())
        started.append((cond, make))

    def both(a, b):
        if a is None:
            return b
        return a if b is None else jnp.logical_and(a, b)

    def halos(cond, s, block):
        launch(
            both(cond, has_below),
            lambda: remote(block, above_ref.at[s], above_send.at[s], above_recv.at[s], me, t + 1),
        )
        launch(
            both(cond, has_above),
            lambda: remote(block, below_ref.at[s], below_send.at[s], below_recv.at[s], me, t - 1),
        )

    def lift(cond, s, part, block):
        launch(
            both(cond, z < deep - 1),
            lambda: remote(
                block, rows_ref.at[s, part], up_send.at[part, s], main_recv.at[part, s],
                me + across, t,
            ),
        )

    def sink(cond, s, part, block):
        launch(
            both(cond, z > 0),
            lambda: remote(
                block, rows_ref.at[s, part], down_send.at[part, s], main_recv.at[part, s],
                me - across, t,
            ),
        )

    def side(cond, s, part, block):
        for j in range(1, across):
            launch(
                cond,
                lambda j=j: remote(
                    block,
                    rows_ref.at[s, part],
                    side_send.at[j - 1, part, s],
                    main_recv.at[part, s],
                    z * across + (x + j) % across,
                    t,
                ),
            )

    def arrive(cond, s, part):
        def wait():
            remote(
                rows_ref.at[s, part], rows_ref.at[s, part], up_send.at[part, s],
                main_recv.at[part, s], me, t,
            ).wait_recv()

        pl.when(cond)(wait) if cond is not None else wait()

    for j in range(1, owners):
        peer = (me + j) % owners
        launch(
            None,
            lambda j=j, peer=peer: remote(
                note_ref.at[peer], noted_ref.at[me], note_send.at[j - 1], note_recv.at[me], peer, t
            ),
        )
    for part in range(2):
        lift(None, me, part, own_ref.at[part])
        sink(None, me, part, own_ref.at[part])
        side(None, me, part, own_ref.at[part])
        if part == 0:
            halos(None, me, own_ref.at[0])
    kept = pltpu.make_async_copy(own_ref, rows_ref.at[me], local_sem.at[0])
    kept.start()
    noted = pltpu.make_async_copy(note_ref.at[me], noted_ref.at[me], local_sem.at[1])
    noted.start()

    def side_arrivals(k, part):
        for sign in (1, -1) if k else (1,):
            zs = z - sign * k
            cond = (zs >= 0 if sign > 0 else zs < deep) if k else None
            for j in range(1, across):
                s = zs * across + (x + j) % across
                arrive(cond, s, part)
                if part == 0:
                    halos(cond, s, rows_ref.at[s, 0])

    for k in range(1, deep):
        lower, upper = z - k, z + k
        for part in range(2):
            for zs, cond, onward in ((lower, lower >= 0, lift), (upper, upper < deep, sink)):
                s = zs * across + x
                arrive(cond, s, part)
                onward(cond, s, part, rows_ref.at[s, part])
                side(cond, s, part, rows_ref.at[s, part])
                if part == 0:
                    halos(cond, s, rows_ref.at[s, 0])
            side_arrivals(k - 1, part)
    for part in range(2):
        side_arrivals(deep - 1, part)

    for j in range(1, owners):
        s = (me + j) % owners
        remote(
            note_ref.at[s], noted_ref.at[s], note_send.at[j - 1], note_recv.at[s], s, t
        ).wait_recv()
    for s in range(owners):
        pl.when(has_above)(
            lambda s=s: remote(
                above_ref.at[s], above_ref.at[s], above_send.at[s], above_recv.at[s], me, t
            ).wait_recv()
        )
        pl.when(has_below)(
            lambda s=s: remote(
                below_ref.at[s], below_ref.at[s], below_send.at[s], below_recv.at[s], me, t
            ).wait_recv()
        )
    for cond, make in started:
        if cond is None:
            make().wait_send()
        else:
            pl.when(cond)(lambda make=make: make().wait_send())
    kept.wait()
    noted.wait()


def spread(own, note, owners, tiles):
    deep, across = grid_of(owners)
    dma = pltpu.SemaphoreType.DMA
    anywhere = pl.BlockSpec(memory_space=pl.ANY)
    return pl.pallas_call(
        functools.partial(spread_kernel, deep, across, tiles),
        out_shape=[
            jax.ShapeDtypeStruct((owners,) + own.shape, own.dtype),
            jax.ShapeDtypeStruct((owners,) + own.shape[1:], own.dtype),
            jax.ShapeDtypeStruct((owners,) + own.shape[1:], own.dtype),
            jax.ShapeDtypeStruct(note.shape, note.dtype),
        ],
        in_specs=[pl.BlockSpec(memory_space=pltpu.VMEM)] * 2,
        out_specs=[anywhere] * 4,
        scratch_shapes=[
            dma((2,)), dma((2, owners)), dma((owners,)), dma((owners,)), dma((owners,)),
            dma((2, owners)), dma((2, owners)), dma((max(across - 1, 1), 2, owners)),
            dma((owners,)), dma((owners,)), dma((owners,)),
        ],
        compiler_params=pltpu.CompilerParams(
            collective_id=0, has_side_effects=True, vmem_limit_bytes=8 * 1024 * 1024
        ),
        name="spread",
    )(own, note)


def collect_kernel(
    deep, across, high, cores,
    terms_ref, gate_ref, bank_ref, own_ref,
    result_ref, input_ref, gated_ref, grad_ref,
    above, below, side_out, side_in, far_out, far_in, total, mate_in, band_out, band_in,
    local_sem, above_send, above_recv, below_send, below_recv,
    side_send, side_recv, far_send, far_recv, mate_send, mate_recv, band_send, band_recv,
    gate_send, gate_recv,
):
    me, t = lax.axis_index("dp"), lax.axis_index("tile")
    z, x = me // across, me % across
    y, core = t // cores, t % cores
    owners, tiles = deep * across, high * cores
    frames = own_ref.shape[1]
    steps = grad_ref.shape[0]
    has_above, has_below = t > 0, t < tiles - 1

    barrier = pltpu.get_barrier_semaphore()
    for j in range(1, owners):
        pl.semaphore_signal(
            barrier, device_id=((me + j) % owners, t), device_id_type=pl.DeviceIdType.MESH
        )
    for j in range(1, tiles):
        pl.semaphore_signal(
            barrier, device_id=(me, (t + j) % tiles), device_id_type=pl.DeviceIdType.MESH
        )
    pl.semaphore_wait(barrier, owners - 1 + tiles - 1)

    started = []

    def launch(make, cond=None):
        if cond is None:
            make().start()
        else:
            pl.when(cond)(lambda: make().start())
        started.append((cond, make))

    ring = [(z + k) % deep for k in list(range(1, deep)) + [0]]

    def lower(s):
        return remote(terms_ref.at[s, 2], above.at[s], above_send.at[s], above_recv.at[s], me, t + 1)

    def upper(s):
        return remote(terms_ref.at[s, 0], below.at[s], below_send.at[s], below_recv.at[s], me, t - 1)

    for j in list(range(1, across)) + [0]:
        for zs in ring:
            s = zs * across + (x + j) % across
            launch(lambda s=s: lower(s), has_below)
            launch(lambda s=s: upper(s), has_above)

    bands = [(y + k) % high for k in list(range(1, high)) + [0]]
    for k, ys in enumerate(bands):
        for j in range(1, cores):
            mate = (core + j) % cores
            launch(
                lambda k=k, j=j, ys=ys, mate=mate: remote(
                    bank_ref.at[ys * cores + mate],
                    mate_in.at[k, j - 1],
                    mate_send.at[k, j - 1],
                    mate_recv.at[k, j - 1],
                    me,
                    y * cores + mate,
                )
            )
    for j in range(1, owners):
        peer = (me + j) % owners
        launch(
            lambda j=j, peer=peer: remote(
                gate_ref.at[peer], gated_ref.at[me], gate_send.at[j - 1], gate_recv.at[j - 1], peer, t
            )
        )
    kept = pltpu.make_async_copy(gate_ref.at[me], gated_ref.at[me], local_sem.at[0])
    kept.start()

    @pl.when(jnp.logical_not(has_above))
    def _():
        above[...] = jnp.zeros_like(above)

    @pl.when(jnp.logical_not(has_below))
    def _():
        below[...] = jnp.zeros_like(below)

    def rims(s):
        pl.when(has_above)(
            lambda: remote(
                above.at[s], above.at[s], above_send.at[s], above_recv.at[s], me, t - 1
            ).wait_recv()
        )
        pl.when(has_below)(
            lambda: remote(
                below.at[s], below.at[s], below_send.at[s], below_recv.at[s], me, t + 1
            ).wait_recv()
        )

    def wide(ref, *at):
        return ref[at].astype(jnp.float32)

    def row(s, f):
        return wide(terms_ref, s, 1, f) + wide(above, s, f) + wide(below, s, f)

    for k, zs in enumerate(ring):
        for j in range(1, across):
            xs = (x + j) % across
            s = zs * across + xs
            rims(s)

            @pl.loop(0, frames)
            def _(f):
                side_out[j - 1, k, 0, f] = row(s, f).astype(jnp.bfloat16)
                side_out[j - 1, k, 1, f] = terms_ref[s, 3, f]

            launch(
                lambda k=k, j=j, xs=xs: remote(
                    side_out.at[j - 1, k],
                    side_in.at[j - 1, k],
                    side_send.at[j - 1, k],
                    side_recv.at[j - 1, k],
                    z * across + xs,
                    t,
                )
            )

    for k, ys in enumerate(bands):
        for j in range(1, cores):
            remote(
                mate_in.at[k, j - 1], mate_in.at[k, j - 1],
                mate_send.at[k, j - 1], mate_recv.at[k, j - 1],
                me, y * cores + (core + j) % cores,
            ).wait_recv()
        if k < high - 1:

            @pl.loop(0, steps)
            def _(i):
                value = wide(bank_ref, ys * cores + core, i)
                for j in range(1, cores):
                    value = value + wide(mate_in, k, j - 1, i)
                band_out[k, i] = value.astype(jnp.bfloat16)

            launch(
                lambda k=k, ys=ys: remote(
                    band_out.at[k], band_in.at[k], band_send.at[k], band_recv.at[k],
                    me, ys * cores + core,
                )
            )

    for k, zs in enumerate(ring):
        s = zs * across + x
        rims(s)
        for j in range(1, across):
            remote(
                side_in.at[j - 1, k], side_in.at[j - 1, k],
                side_send.at[j - 1, k], side_recv.at[j - 1, k],
                z * across + (x + j) % across, t,
            ).wait_recv()

        def summed(f):
            first, second = row(s, f), wide(terms_ref, s, 3, f)
            for j in range(1, across):
                first = first + wide(side_in, j - 1, k, 0, f)
                second = second + wide(side_in, j - 1, k, 1, f)
            return first, second

        if k < deep - 1:

            @pl.loop(0, frames)
            def _(f):
                first, second = summed(f)
                far_out[k, 0, f] = first.astype(jnp.bfloat16)
                far_out[k, 1, f] = second.astype(jnp.bfloat16)

            launch(
                lambda k=k, zs=zs: remote(
                    far_out.at[k], far_in.at[k], far_send.at[k], far_recv.at[k],
                    zs * across + x, t,
                )
            )
        else:

            @pl.loop(0, frames)
            def _(f):
                first, second = summed(f)
                total[0, f] = wide(own_ref, 1, f) + first
                total[1, f] = wide(own_ref, 0, f) + second

    for k in range(high - 1):
        remote(
            band_in.at[k], band_in.at[k], band_send.at[k], band_recv.at[k],
            me, bands[k] * cores + core,
        ).wait_recv()

    @pl.loop(0, steps)
    def _(i):
        value = wide(bank_ref, t, i)
        for j in range(1, cores):
            value = value + wide(mate_in, high - 1, j - 1, i)
        for k in range(high - 1):
            value = value + wide(band_in, k, i)
        grad_ref[i] = value

    for k in range(deep - 1):
        remote(
            far_in.at[k], far_in.at[k], far_send.at[k], far_recv.at[k], ring[k] * across + x, t
        ).wait_recv()

    @pl.loop(0, frames)
    def _(f):
        first, second = total[0, f], total[1, f]
        for k in range(deep - 1):
            first = first + wide(far_in, k, 0, f)
            second = second + wide(far_in, k, 1, f)
        input_ref[f] = first.astype(jnp.bfloat16)
        result_ref[f] = second.astype(jnp.bfloat16)

    for j in range(1, owners):
        s = (me + owners - j) % owners
        remote(
            gate_ref.at[s], gated_ref.at[s], gate_send.at[j - 1], gate_recv.at[j - 1], s, t
        ).wait_recv()
    for cond, make in started:
        if cond is None:
            make().wait_send()
        else:
            pl.when(cond)(lambda make=make: make().wait_send())
    kept.wait()


def collect(terms, gates, bank, own):
    owners, _, frames, columns, channels = terms.shape
    tiles, steps, share, _ = bank.shape
    deep, across = grid_of(owners)
    cores = 1 if tiles % 2 else 2
    high = tiles // cores
    dma = pltpu.SemaphoreType.DMA
    vmem = pl.BlockSpec(memory_space=pltpu.VMEM)
    beside, past, mates, far = (max(v - 1, 1) for v in (across, deep, cores, high))
    block = (2, frames, columns, channels)

    def room(*shape):
        return pltpu.VMEM(shape, jnp.bfloat16)

    return pl.pallas_call(
        functools.partial(collect_kernel, deep, across, high, cores),
        out_shape=[
            jax.ShapeDtypeStruct(block[1:], jnp.bfloat16),
            jax.ShapeDtypeStruct(block[1:], jnp.bfloat16),
            jax.ShapeDtypeStruct(gates.shape, gates.dtype),
            jax.ShapeDtypeStruct(bank.shape[1:], jnp.float32),
        ],
        in_specs=[vmem] * 4,
        out_specs=[vmem] * 4,
        scratch_shapes=[
            room(owners, *block[1:]),
            room(owners, *block[1:]),
            room(beside, deep, *block),
            room(beside, deep, *block),
            room(past, *block),
            room(past, *block),
            pltpu.VMEM(block, jnp.float32),
            room(high, mates, steps, share, channels),
            room(far, steps, share, channels),
            room(far, steps, share, channels),
            dma((1,)),
            dma((owners,)), dma((owners,)), dma((owners,)), dma((owners,)),
            dma((beside, deep)), dma((beside, deep)),
            dma((past,)), dma((past,)),
            dma((high, mates)), dma((high, mates)),
            dma((far,)), dma((far,)),
            dma((max(owners - 1, 1),)), dma((max(owners - 1, 1),)),
        ],
        compiler_params=pltpu.CompilerParams(
            collective_id=1, has_side_effects=True, vmem_limit_bytes=56 * 1024 * 1024
        ),
        name="collect",
    )(terms, gates, bank, own)


def shards(frames, kernels, experts, counts, gate_weights, cotangent):
    owners = lax.axis_size("dp")
    tiles = lax.axis_size("tile")
    local = kernels.shape[0]
    chosen = experts[:, 0]
    frame_count, slots = chosen.shape
    active = jnp.arange(slots)[None, :] < counts[:, 0][:, None]
    owner_of = chosen // local
    hit = (owner_of[:, :, None] == jnp.arange(owners)) & active[:, :, None]
    wanted = jnp.any(hit, axis=1)
    position = jnp.cumsum(wanted.astype(jnp.int32), axis=0) - 1
    slot_map = wanted.T[:, None, :] & (
        position.T[:, None, :] == jnp.arange(CAP)[None, :, None]
    )
    request = jnp.max(jnp.where(hit, (chosen % local)[:, :, None], 0), axis=(0, 1))
    tile_gate = jnp.sum(jnp.where(hit, gate_weights[:, 0][:, :, None], 0.0), axis=1)
    weight = jnp.sum(jnp.where(slot_map, tile_gate.T[:, None, :], 0.0), axis=2)
    place = jnp.sum(
        jnp.where(slot_map, jnp.arange(frame_count)[None, None, :], 0), axis=2
    )
    note = jnp.concatenate(
        [request[:, None].astype(jnp.float32), weight, place.astype(jnp.float32)], axis=1
    )
    note = jnp.pad(note[:, None, :], ((0, 0), (0, 7), (0, 128 - note.shape[1])))
    own = jnp.stack([frames[:, 0], cotangent[:, 0]])
    rows, above, below, noted = spread(own, note, owners, tiles)
    noted = noted[:, 0]
    pick = noted[:, 0].astype(jnp.int32)
    shares = noted[:, 1 : 1 + CAP]
    places = noted[:, 1 + CAP : 1 + 2 * CAP].astype(jnp.int32)
    t = lax.axis_index("tile")
    rim = jnp.stack([t > 0, t < tiles - 1]).astype(jnp.int32)

    back, gates, bank_grad = owner(
        pick, shares, places, rim, rows, above, below, kernels, tiles
    )
    result, input_grad, gated, bank_part = collect(back, gates, bank_grad, own)
    kernel_part = jnp.swapaxes(bank_part, 1, 2).reshape(
        kernels.shape[:3] + (bank_part.shape[1],)
    )
    gated = gated[:, :CAP, 0]
    selected = jnp.sum(jnp.where(slot_map, gated[:, :, None], 0.0), axis=1)
    gate_grad = jnp.sum(jnp.where(hit, selected.T[:, None, :], 0.0), axis=2)
    return (result[:, None], input_grad[:, None], gate_grad[:, None, :], kernel_part)


def solution(mesh):
    return jax.shard_map(
        shards,
        mesh=mesh,
        in_specs=(
            P("dp", "tile", None, None),
            P("dp", None, None, None),
            P("dp", "tile", None),
            P("dp", "tile"),
            P("dp", "tile", None),
            P("dp", "tile", None, None),
        ),
        out_specs=(
            P("dp", "tile", None, None),
            P("dp", "tile", None, None),
            P("dp", "tile", None),
            P("dp", None, None, "tile"),
        ),
        check_vma=False,
    )
```

```python
import functools

import jax
import jax.numpy as jnp
from jax import lax
from jax.experimental import pallas as pl
from jax.experimental.pallas import tpu as pltpu
from jax.sharding import PartitionSpec as P

CAP = 2


def shifts(columns, rows):
    place = lax.broadcasted_iota(jnp.int32, (rows, 1), 0) % columns

    def later(v):
        return jnp.where(place == 0, 0.0, pltpu.roll(v, 1, 0))

    def sooner(v):
        return jnp.where(place == columns - 1, 0.0, pltpu.roll(v, rows - 1, 0))

    return later, sooner


def owner_kernel(
    pick_ref, weight_ref, place_ref, rim_ref,
    rows_ref, above_ref, below_ref, bank_ref, back_ref, edge_ref, gate_ref, out_ref, grad_ref,
):
    s = pl.program_id(0)
    cap = CAP
    columns, channels = back_ref.shape[3:]
    steps = out_ref.shape[1]
    rows = cap * columns
    later, sooner = shifts(columns, rows)

    @pl.when(s == 0)
    def _():
        @pl.loop(0, steps)
        def _(i):
            grad_ref[:, i] = jnp.zeros_like(grad_ref[:, i])

    back_ref[...] = jnp.zeros_like(back_ref)

    item = lax.broadcasted_iota(jnp.int32, (rows, 1), 0) // columns
    weight = jnp.zeros((rows, 1), jnp.float32)
    for c in range(cap):
        weight = jnp.where(item == c, weight_ref[s, c], weight)

    def gather(ref, *lead):
        return jnp.concatenate([ref[(0,) + lead + (place_ref[s, c],)] for c in range(cap)], axis=0)

    blank = jnp.zeros((rows, channels), jnp.bfloat16)
    window = [
        jnp.where(rim_ref[0] > 0, gather(above_ref), blank),
        gather(rows_ref, 0),
        jnp.where(rim_ref[1] > 0, gather(below_ref), blank),
    ]
    upstream = gather(rows_ref, 1).astype(jnp.float32)

    def column_term(db):
        total = jnp.dot(window[0], bank_ref[0, db], preferred_element_type=jnp.float32)
        for da in (1, 2):
            total = total + jnp.dot(
                window[da], bank_ref[0, 3 * da + db], preferred_element_type=jnp.float32
            )
        return total

    pre = column_term(1) + later(column_term(0)) + sooner(column_term(2))
    pre = pre.astype(jnp.bfloat16).astype(jnp.float32)
    squash = jax.nn.sigmoid(pre)
    activated = pre * squash
    slope = squash * (1.0 + pre * (1.0 - squash))

    def put(r, value):
        value = value.astype(jnp.bfloat16).reshape(cap, columns, channels)
        for c in reversed(range(cap)):
            back_ref[0, r, place_ref[s, c]] = value[c]

    put(1, weight * activated)
    gates = jnp.sum((upstream * activated).reshape(cap, columns, channels), axis=1)
    gates = jnp.broadcast_to(jnp.sum(gates, axis=1, keepdims=True), (cap, 128))
    gate_ref[0] = jnp.concatenate([gates, jnp.zeros((8 - cap, 128), jnp.float32)], axis=0)

    grad = (upstream * weight * slope).astype(jnp.bfloat16)
    for da in range(3):
        parts = [
            lax.dot_general(
                grad,
                bank_ref[0, 3 * da + db],
                (((1,), (1,)), ((), ())),
                preferred_element_type=jnp.float32,
            )
            for db in range(3)
        ]
        total = parts[1] + sooner(parts[0]) + later(parts[2])
        if da == 1:
            put(0, total)
        else:
            edge_ref[0, da // 2] = total.astype(jnp.bfloat16).reshape(cap, columns, channels)

    grad_wide = grad.astype(jnp.float32)
    moved = [sooner(grad_wide).astype(jnp.bfloat16), grad, later(grad_wide).astype(jnp.bfloat16)]
    e = pick_ref[s]
    chunks, _, share, _ = grad_ref.shape
    taps = bank_ref.shape[1]
    for db in range(3):
        for da in range(3):
            term = lax.dot_general(
                moved[db], window[da], (((0,), (0,)), ((), ())), preferred_element_type=jnp.float32
            )
            grad_ref[:, e * taps + 3 * da + db] += term.reshape(chunks, share, channels)

    @pl.when(s == pl.num_programs(0) - 1)
    def _():
        @pl.loop(0, steps)
        def _(i):
            out_ref[:, i] = grad_ref[:, i].astype(out_ref.dtype)


def owner(pick, weight, place, rim, rows, above, below, kernels, chunks):
    sources, _, frames, columns, channels = rows.shape
    experts, taps, _, outputs = kernels.shape
    spec = pltpu.PrefetchScalarGridSpec(
        num_scalar_prefetch=4,
        grid=(sources,),
        in_specs=[
            pl.BlockSpec((1, 2, frames, columns, channels), lambda s, *_: (s, 0, 0, 0, 0)),
            pl.BlockSpec((1, frames, columns, channels), lambda s, *_: (s, 0, 0, 0)),
            pl.BlockSpec((1, frames, columns, channels), lambda s, *_: (s, 0, 0, 0)),
            pl.BlockSpec((1, taps, channels, outputs), lambda s, p, *_: (p[s], 0, 0, 0)),
        ],
        out_specs=[
            pl.BlockSpec((1, 2, frames, columns, channels), lambda s, *_: (s, 0, 0, 0, 0)),
            pl.BlockSpec((1, 2, CAP, columns, channels), lambda s, *_: (s, 0, 0, 0, 0)),
            pl.BlockSpec((1, 8, 128), lambda s, *_: (s, 0, 0)),
            pl.BlockSpec(
                (chunks, experts * taps, outputs // chunks, channels),
                lambda s, *_: (0, 0, 0, 0),
                pipeline_mode=pl.Buffered(1),
            ),
        ],
        scratch_shapes=[
            pltpu.VMEM((chunks, experts * taps, outputs // chunks, channels), jnp.float32)
        ],
    )
    return pl.pallas_call(
        owner_kernel,
        grid_spec=spec,
        out_shape=[
            jax.ShapeDtypeStruct((sources, 2, frames, columns, channels), jnp.bfloat16),
            jax.ShapeDtypeStruct((sources, 2, CAP, columns, channels), jnp.bfloat16),
            jax.ShapeDtypeStruct((sources, 8, 128), jnp.float32),
            jax.ShapeDtypeStruct(
                (chunks, experts * taps, outputs // chunks, channels), jnp.bfloat16
            ),
        ],
        compiler_params=pltpu.CompilerParams(vmem_limit_bytes=48 * 1024 * 1024),
        name="owner",
    )(pick, weight, place, rim, rows, above, below, kernels)


def grid_of(owners):
    across = 1
    while across * across * 4 <= owners:
        across *= 2
    while owners % across:
        across -= 1
    return owners // across, across


def remote(src, dst, send, recv, dp, tile):
    return pltpu.make_async_remote_copy(
        src_ref=src,
        dst_ref=dst,
        send_sem=send,
        recv_sem=recv,
        device_id=(dp, tile),
        device_id_type=pl.DeviceIdType.MESH,
    )


def spread_kernel(
    deep, across, tiles,
    own_ref, note_ref, rows_ref, above_ref, below_ref, noted_ref,
    local_sem, main_recv, above_recv, below_recv, note_recv,
    up_send, down_send, side_send, above_send, below_send, note_send,
):
    me, t = lax.axis_index("dp"), lax.axis_index("tile")
    z, x = me // across, me % across
    owners = deep * across
    has_above, has_below = t > 0, t < tiles - 1

    barrier = pltpu.get_barrier_semaphore()

    def greet(dp, tile):
        pl.semaphore_signal(
            barrier, inc=1, device_id=(dp, tile), device_id_type=pl.DeviceIdType.MESH
        )

    for j in range(1, owners):
        greet((me + j) % owners, t)
    pl.when(has_above)(lambda: greet(me, t - 1))
    pl.when(has_below)(lambda: greet(me, t + 1))
    pl.semaphore_wait(
        barrier, owners - 1 + has_above.astype(jnp.int32) + has_below.astype(jnp.int32)
    )

    started = []

    def launch(cond, make):
        if cond is None:
            make().start()
        else:
            pl.when(cond)(lambda: make().start())
        started.append((cond, make))

    def both(a, b):
        if a is None:
            return b
        return a if b is None else jnp.logical_and(a, b)

    def halos(cond, s, block):
        launch(
            both(cond, has_below),
            lambda: remote(block, above_ref.at[s], above_send.at[s], above_recv.at[s], me, t + 1),
        )
        launch(
            both(cond, has_above),
            lambda: remote(block, below_ref.at[s], below_send.at[s], below_recv.at[s], me, t - 1),
        )

    def lift(cond, s, part, block):
        launch(
            both(cond, z < deep - 1),
            lambda: remote(
                block, rows_ref.at[s, part], up_send.at[part, s], main_recv.at[part, s],
                me + across, t,
            ),
        )

    def sink(cond, s, part, block):
        launch(
            both(cond, z > 0),
            lambda: remote(
                block, rows_ref.at[s, part], down_send.at[part, s], main_recv.at[part, s],
                me - across, t,
            ),
        )

    def side(cond, s, part, block):
        for j in range(1, across):
            launch(
                cond,
                lambda j=j: remote(
                    block,
                    rows_ref.at[s, part],
                    side_send.at[j - 1, part, s],
                    main_recv.at[part, s],
                    z * across + (x + j) % across,
                    t,
                ),
            )

    def arrive(cond, s, part):
        def wait():
            remote(
                rows_ref.at[s, part], rows_ref.at[s, part], up_send.at[part, s],
                main_recv.at[part, s], me, t,
            ).wait_recv()

        pl.when(cond)(wait) if cond is not None else wait()

    for j in range(1, owners):
        peer = (me + j) % owners
        launch(
            None,
            lambda j=j, peer=peer: remote(
                note_ref.at[peer], noted_ref.at[me], note_send.at[j - 1], note_recv.at[me], peer, t
            ),
        )
    for part in range(2):
        lift(None, me, part, own_ref.at[part])
        sink(None, me, part, own_ref.at[part])
        side(None, me, part, own_ref.at[part])
        if part == 0:
            halos(None, me, own_ref.at[0])
    kept = pltpu.make_async_copy(own_ref, rows_ref.at[me], local_sem.at[0])
    kept.start()
    noted = pltpu.make_async_copy(note_ref.at[me], noted_ref.at[me], local_sem.at[1])
    noted.start()

    def side_arrivals(k, part):
        for sign in (1, -1) if k else (1,):
            zs = z - sign * k
            cond = (zs >= 0 if sign > 0 else zs < deep) if k else None
            for j in range(1, across):
                s = zs * across + (x + j) % across
                arrive(cond, s, part)
                if part == 0:
                    halos(cond, s, rows_ref.at[s, 0])

    for k in range(1, deep):
        lower, upper = z - k, z + k
        for part in range(2):
            for zs, cond, onward in ((lower, lower >= 0, lift), (upper, upper < deep, sink)):
                s = zs * across + x
                arrive(cond, s, part)
                onward(cond, s, part, rows_ref.at[s, part])
                side(cond, s, part, rows_ref.at[s, part])
                if part == 0:
                    halos(cond, s, rows_ref.at[s, 0])
            side_arrivals(k - 1, part)
    for part in range(2):
        side_arrivals(deep - 1, part)

    for j in range(1, owners):
        s = (me + j) % owners
        remote(
            note_ref.at[s], noted_ref.at[s], note_send.at[j - 1], note_recv.at[s], s, t
        ).wait_recv()
    for s in range(owners):
        pl.when(has_above)(
            lambda s=s: remote(
                above_ref.at[s], above_ref.at[s], above_send.at[s], above_recv.at[s], me, t
            ).wait_recv()
        )
        pl.when(has_below)(
            lambda s=s: remote(
                below_ref.at[s], below_ref.at[s], below_send.at[s], below_recv.at[s], me, t
            ).wait_recv()
        )
    for cond, make in started:
        if cond is None:
            make().wait_send()
        else:
            pl.when(cond)(lambda make=make: make().wait_send())
    kept.wait()
    noted.wait()


def spread(own, note, owners, tiles):
    deep, across = grid_of(owners)
    dma = pltpu.SemaphoreType.DMA
    anywhere = pl.BlockSpec(memory_space=pl.ANY)
    return pl.pallas_call(
        functools.partial(spread_kernel, deep, across, tiles),
        out_shape=[
            jax.ShapeDtypeStruct((owners,) + own.shape, own.dtype),
            jax.ShapeDtypeStruct((owners,) + own.shape[1:], own.dtype),
            jax.ShapeDtypeStruct((owners,) + own.shape[1:], own.dtype),
            jax.ShapeDtypeStruct(note.shape, note.dtype),
        ],
        in_specs=[pl.BlockSpec(memory_space=pltpu.VMEM)] * 2,
        out_specs=[anywhere] * 4,
        scratch_shapes=[
            dma((2,)), dma((2, owners)), dma((owners,)), dma((owners,)), dma((owners,)),
            dma((2, owners)), dma((2, owners)), dma((max(across - 1, 1), 2, owners)),
            dma((owners,)), dma((owners,)), dma((owners,)),
        ],
        compiler_params=pltpu.CompilerParams(
            collective_id=0, has_side_effects=True, vmem_limit_bytes=8 * 1024 * 1024
        ),
        name="spread",
    )(own, note)


def collect_kernel(
    deep, across, high, cores,
    terms_ref, edge_ref, note_ref, gate_ref, bank_ref, own_ref,
    result_ref, input_ref, gated_ref, grad_ref,
    above, below, above_note, below_note, side_out, side_in, far_out, far_in, total, mate_in, band_out, band_in,
    local_sem, above_send, above_recv, below_send, below_recv,
    side_send, side_recv, far_send, far_recv, mate_send, mate_recv, band_send, band_recv,
    gate_send, gate_recv, tell_send, tell_recv,
):
    me, t = lax.axis_index("dp"), lax.axis_index("tile")
    z, x = me // across, me % across
    y, core = t // cores, t % cores
    owners, tiles = deep * across, high * cores
    frames = own_ref.shape[1]
    steps = grad_ref.shape[0]
    has_above, has_below = t > 0, t < tiles - 1

    barrier = pltpu.get_barrier_semaphore()
    for j in range(1, owners):
        pl.semaphore_signal(
            barrier, device_id=((me + j) % owners, t), device_id_type=pl.DeviceIdType.MESH
        )
    for j in range(1, tiles):
        pl.semaphore_signal(
            barrier, device_id=(me, (t + j) % tiles), device_id_type=pl.DeviceIdType.MESH
        )
    pl.semaphore_wait(barrier, owners - 1 + tiles - 1)

    started = []

    def launch(make, cond=None):
        if cond is None:
            make().start()
        else:
            pl.when(cond)(lambda: make().start())
        started.append((cond, make))

    ring = [(z + k) % deep for k in list(range(1, deep)) + [0]]

    def lower(s):
        return remote(edge_ref.at[s, 1], above.at[s], above_send.at[s], above_recv.at[s], me, t + 1)

    def upper(s):
        return remote(edge_ref.at[s, 0], below.at[s], below_send.at[s], below_recv.at[s], me, t - 1)

    def tell_lower():
        return remote(note_ref, above_note, tell_send.at[0], tell_recv.at[0], me, t + 1)

    def tell_upper():
        return remote(note_ref, below_note, tell_send.at[1], tell_recv.at[1], me, t - 1)

    launch(tell_lower, has_below)
    launch(tell_upper, has_above)
    for j in list(range(1, across)) + [0]:
        for zs in ring:
            s = zs * across + (x + j) % across
            launch(lambda s=s: lower(s), has_below)
            launch(lambda s=s: upper(s), has_above)

    bands = [(y + k) % high for k in list(range(1, high)) + [0]]
    for k, ys in enumerate(bands):
        for j in range(1, cores):
            mate = (core + j) % cores
            launch(
                lambda k=k, j=j, ys=ys, mate=mate: remote(
                    bank_ref.at[ys * cores + mate],
                    mate_in.at[k, j - 1],
                    mate_send.at[k, j - 1],
                    mate_recv.at[k, j - 1],
                    me,
                    y * cores + mate,
                )
            )
    for j in range(1, owners):
        peer = (me + j) % owners
        launch(
            lambda j=j, peer=peer: remote(
                gate_ref.at[peer], gated_ref.at[me], gate_send.at[j - 1], gate_recv.at[j - 1], peer, t
            )
        )
    kept = pltpu.make_async_copy(gate_ref.at[me], gated_ref.at[me], local_sem.at[0])
    kept.start()

    @pl.when(jnp.logical_not(has_above))
    def _():
        above[...] = jnp.zeros_like(above)
        above_note[...] = jnp.zeros_like(above_note)

    @pl.when(jnp.logical_not(has_below))
    def _():
        below[...] = jnp.zeros_like(below)
        below_note[...] = jnp.zeros_like(below_note)

    pl.when(has_above)(
        lambda: remote(
            above_note, above_note, tell_send.at[0], tell_recv.at[0], me, t - 1
        ).wait_recv()
    )
    pl.when(has_below)(
        lambda: remote(
            below_note, below_note, tell_send.at[1], tell_recv.at[1], me, t + 1
        ).wait_recv()
    )

    def rims(s):
        pl.when(has_above)(
            lambda: remote(
                above.at[s], above.at[s], above_send.at[s], above_recv.at[s], me, t - 1
            ).wait_recv()
        )
        pl.when(has_below)(
            lambda: remote(
                below.at[s], below.at[s], below_send.at[s], below_recv.at[s], me, t + 1
            ).wait_recv()
        )

    def wide(ref, *at):
        return ref[at].astype(jnp.float32)

    def row(s, f):
        value = wide(terms_ref, s, 0, f)
        for note, items in ((above_note, above), (below_note, below)):
            for c in range(CAP):
                place = note[s, c : c + 1, :]
                place = jnp.concatenate([place] * (value.shape[1] // place.shape[1]), axis=1)
                here = jnp.broadcast_to(place, value.shape) == f.astype(jnp.float32)
                value = value + jnp.where(here, wide(items, s, c), 0.0)
        return value

    for k, zs in enumerate(ring):
        for j in range(1, across):
            xs = (x + j) % across
            s = zs * across + xs
            rims(s)

            @pl.loop(0, frames)
            def _(f):
                side_out[j - 1, k, 0, f] = row(s, f).astype(jnp.bfloat16)
                side_out[j - 1, k, 1, f] = terms_ref[s, 1, f]

            launch(
                lambda k=k, j=j, xs=xs: remote(
                    side_out.at[j - 1, k],
                    side_in.at[j - 1, k],
                    side_send.at[j - 1, k],
                    side_recv.at[j - 1, k],
                    z * across + xs,
                    t,
                )
            )

    for k, ys in enumerate(bands):
        for j in range(1, cores):
            remote(
                mate_in.at[k, j - 1], mate_in.at[k, j - 1],
                mate_send.at[k, j - 1], mate_recv.at[k, j - 1],
                me, y * cores + (core + j) % cores,
            ).wait_recv()
        if k < high - 1:

            @pl.loop(0, steps)
            def _(i):
                value = wide(bank_ref, ys * cores + core, i)
                for j in range(1, cores):
                    value = value + wide(mate_in, k, j - 1, i)
                band_out[k, i] = value.astype(jnp.bfloat16)

            launch(
                lambda k=k, ys=ys: remote(
                    band_out.at[k], band_in.at[k], band_send.at[k], band_recv.at[k],
                    me, ys * cores + core,
                )
            )

    for k, zs in enumerate(ring):
        s = zs * across + x
        rims(s)
        for j in range(1, across):
            remote(
                side_in.at[j - 1, k], side_in.at[j - 1, k],
                side_send.at[j - 1, k], side_recv.at[j - 1, k],
                z * across + (x + j) % across, t,
            ).wait_recv()

        def summed(f):
            first, second = row(s, f), wide(terms_ref, s, 1, f)
            for j in range(1, across):
                first = first + wide(side_in, j - 1, k, 0, f)
                second = second + wide(side_in, j - 1, k, 1, f)
            return first, second

        if k < deep - 1:

            @pl.loop(0, frames)
            def _(f):
                first, second = summed(f)
                far_out[k, 0, f] = first.astype(jnp.bfloat16)
                far_out[k, 1, f] = second.astype(jnp.bfloat16)

            launch(
                lambda k=k, zs=zs: remote(
                    far_out.at[k], far_in.at[k], far_send.at[k], far_recv.at[k],
                    zs * across + x, t,
                )
            )
        else:

            @pl.loop(0, frames)
            def _(f):
                first, second = summed(f)
                total[0, f] = wide(own_ref, 1, f) + first
                total[1, f] = wide(own_ref, 0, f) + second

    for k in range(high - 1):
        remote(
            band_in.at[k], band_in.at[k], band_send.at[k], band_recv.at[k],
            me, bands[k] * cores + core,
        ).wait_recv()

    @pl.loop(0, steps)
    def _(i):
        value = wide(bank_ref, t, i)
        for j in range(1, cores):
            value = value + wide(mate_in, high - 1, j - 1, i)
        for k in range(high - 1):
            value = value + wide(band_in, k, i)
        grad_ref[i] = value

    for k in range(deep - 1):
        remote(
            far_in.at[k], far_in.at[k], far_send.at[k], far_recv.at[k], ring[k] * across + x, t
        ).wait_recv()

    @pl.loop(0, frames)
    def _(f):
        first, second = total[0, f], total[1, f]
        for k in range(deep - 1):
            first = first + wide(far_in, k, 0, f)
            second = second + wide(far_in, k, 1, f)
        input_ref[f] = first.astype(jnp.bfloat16)
        result_ref[f] = second.astype(jnp.bfloat16)

    for j in range(1, owners):
        s = (me + owners - j) % owners
        remote(
            gate_ref.at[s], gated_ref.at[s], gate_send.at[j - 1], gate_recv.at[j - 1], s, t
        ).wait_recv()
    for cond, make in started:
        if cond is None:
            make().wait_send()
        else:
            pl.when(cond)(lambda make=make: make().wait_send())
    kept.wait()


def collect(terms, edges, notes, gates, bank, own):
    owners, _, frames, columns, channels = terms.shape
    tiles, steps, share, _ = bank.shape
    deep, across = grid_of(owners)
    cores = 1 if tiles % 2 else 2
    high = tiles // cores
    dma = pltpu.SemaphoreType.DMA
    vmem = pl.BlockSpec(memory_space=pltpu.VMEM)
    beside, past, mates, far = (max(v - 1, 1) for v in (across, deep, cores, high))
    block = (2, frames, columns, channels)

    def room(*shape):
        return pltpu.VMEM(shape, jnp.bfloat16)

    return pl.pallas_call(
        functools.partial(collect_kernel, deep, across, high, cores),
        out_shape=[
            jax.ShapeDtypeStruct(block[1:], jnp.bfloat16),
            jax.ShapeDtypeStruct(block[1:], jnp.bfloat16),
            jax.ShapeDtypeStruct(gates.shape, gates.dtype),
            jax.ShapeDtypeStruct(bank.shape[1:], jnp.float32),
        ],
        in_specs=[vmem] * 6,
        out_specs=[vmem] * 4,
        scratch_shapes=[
            room(owners, *edges.shape[2:]),
            room(owners, *edges.shape[2:]),
            pltpu.VMEM(notes.shape, jnp.float32),
            pltpu.VMEM(notes.shape, jnp.float32),
            room(beside, deep, *block),
            room(beside, deep, *block),
            room(past, *block),
            room(past, *block),
            pltpu.VMEM(block, jnp.float32),
            room(high, mates, steps, share, channels),
            room(far, steps, share, channels),
            room(far, steps, share, channels),
            dma((1,)),
            dma((owners,)), dma((owners,)), dma((owners,)), dma((owners,)),
            dma((beside, deep)), dma((beside, deep)),
            dma((past,)), dma((past,)),
            dma((high, mates)), dma((high, mates)),
            dma((far,)), dma((far,)),
            dma((max(owners - 1, 1),)), dma((max(owners - 1, 1),)),
            dma((2,)), dma((2,)),
        ],
        compiler_params=pltpu.CompilerParams(
            collective_id=1, has_side_effects=True, vmem_limit_bytes=56 * 1024 * 1024
        ),
        name="collect",
    )(terms, edges, notes, gates, bank, own)


def shards(frames, kernels, experts, counts, gate_weights, cotangent):
    owners = lax.axis_size("dp")
    tiles = lax.axis_size("tile")
    local = kernels.shape[0]
    chosen = experts[:, 0]
    frame_count, slots = chosen.shape
    active = jnp.arange(slots)[None, :] < counts[:, 0][:, None]
    owner_of = chosen // local
    hit = (owner_of[:, :, None] == jnp.arange(owners)) & active[:, :, None]
    wanted = jnp.any(hit, axis=1)
    position = jnp.cumsum(wanted.astype(jnp.int32), axis=0) - 1
    slot_map = wanted.T[:, None, :] & (
        position.T[:, None, :] == jnp.arange(CAP)[None, :, None]
    )
    request = jnp.max(jnp.where(hit, (chosen % local)[:, :, None], 0), axis=(0, 1))
    tile_gate = jnp.sum(jnp.where(hit, gate_weights[:, 0][:, :, None], 0.0), axis=1)
    weight = jnp.sum(jnp.where(slot_map, tile_gate.T[:, None, :], 0.0), axis=2)
    place = jnp.sum(
        jnp.where(slot_map, jnp.arange(frame_count)[None, None, :], 0), axis=2
    )
    note = jnp.concatenate(
        [request[:, None].astype(jnp.float32), weight, place.astype(jnp.float32)], axis=1
    )
    note = jnp.pad(note[:, None, :], ((0, 0), (0, 7), (0, 128 - note.shape[1])))
    own = jnp.stack([frames[:, 0], cotangent[:, 0]])
    rows, above, below, noted = spread(own, note, owners, tiles)
    noted = noted[:, 0]
    pick = noted[:, 0].astype(jnp.int32)
    shares = noted[:, 1 : 1 + CAP]
    places = noted[:, 1 + CAP : 1 + 2 * CAP].astype(jnp.int32)
    t = lax.axis_index("tile")
    rim = jnp.stack([t > 0, t < tiles - 1]).astype(jnp.int32)

    spots = jnp.broadcast_to(places.astype(jnp.float32)[:, :, None], (owners, CAP, 128))
    spots = jnp.pad(spots, ((0, 0), (0, 8 - CAP), (0, 0)))
    back, edges, gates, bank_grad = owner(
        pick, shares, places, rim, rows, above, below, kernels, tiles
    )
    result, input_grad, gated, bank_part = collect(back, edges, spots, gates, bank_grad, own)
    kernel_part = jnp.swapaxes(bank_part, 1, 2).reshape(
        kernels.shape[:3] + (bank_part.shape[1],)
    )
    gated = gated[:, :CAP, 0]
    selected = jnp.sum(jnp.where(slot_map, gated[:, :, None], 0.0), axis=1)
    gate_grad = jnp.sum(jnp.where(hit, selected.T[:, None, :], 0.0), axis=2)
    return (result[:, None], input_grad[:, None], gate_grad[:, None, :], kernel_part)


def solution(mesh):
    return jax.shard_map(
        shards,
        mesh=mesh,
        in_specs=(
            P("dp", "tile", None, None),
            P("dp", None, None, None),
            P("dp", "tile", None),
            P("dp", "tile"),
            P("dp", "tile", None),
            P("dp", "tile", None, None),
        ),
        out_specs=(
            P("dp", "tile", None, None),
            P("dp", "tile", None, None),
            P("dp", "tile", None),
            P("dp", None, None, "tile"),
        ),
        check_vma=False,
    )
```
